128 devices in a mesh: bx: 8 (over y_hi, z), by: 16 (over x, y_lo, core).
Axes of the slice: x: 4, y: 4 (y_hi: 2, y_lo: 2; y = y_hi * 2 + y_lo), z: 4, core: 2. Of those that a mesh axis runs over, the one named last changes fastest.
Arguments:
- state: float32 [384, 64, 2048], P(None, 'bx', 'by'), may hold values from -6 to 6
- target: bfloat16 [384, 64, 2048], P(None, 'bx', 'by'), may hold values from -6 to 6
- land_mask: int32 [64, 2048], P('bx', 'by'), may hold values 0 or 1
- batch_map: int32 [64, 2048], P('bx', 'by'), may hold values from 0 to 63
- diffusion: float32 [384], replicated, may hold values from 0.05 to 0.2
- speed_x: float32 [384], replicated, may hold values from -0.3 to 0.3
- speed_y: float32 [384], replicated, may hold values from -0.3 to 0.3
- w_in: bfloat16 [384, 4096], replicated, may hold values from -0.3125 to 0.3125
- w_out: bfloat16 [4096, 384], replicated, may hold values from -0.09375 to 0.09375
Outputs:
- new_state: float32 [384, 64, 2048], P(None, 'bx', 'by')
- grad_in: float32 [4096, 384], P(('bx', 'by'))
- grad_out: float32 [4096, 384], P(('bx', 'by'))
- batch_loss: float32 [64], replicated
The draws below stay inside these ranges and needn't reach their ends.
All inputs are finite; a program needn't handle non-finite values. No bound on the sum of `land_mask` on one device may be relied on, other than what follows from the above.
Results may differ from the reference program's by a relative error of at most 0.0017.
Values sent between devices are 32-bit elements; how exact they have to be, the bound alone decides.
No kernel may reach another device: no remote copies, remote signals or barrier semaphores. Data moves between devices by JAX's collectives and lax.ppermute only.
A program may use at most 128 MiB of HBM per device.

```python
import jax
import jax.numpy as jnp
from jax import lax

HID = 4096
SUB = 3
BATCHES = 64
V = 384
NX = 64
NY = 2048


def touch_ends(values, key, smallest, top_value):
    extent = values.shape
    spot = [jax.random.randint(jax.random.fold_in(key, axis), (), 0, extent[axis]) for axis in range(len(extent))]
    values = values.at[tuple(spot)].set(smallest)
    longest = extent.index(max(extent))
    spot[longest] = (spot[longest] + 1) % extent[longest]
    return values.at[tuple(spot)].set(top_value)


def block_levels(stream_key, extent, shards, smallest, top_value):
    def one(axis_at, shards_of):
        heights = jax.random.uniform(jax.random.fold_in(jax.random.fold_in(stream_key, 6), axis_at), (shards_of,), jnp.float32, smallest / len(shards), top_value / len(shards))
        return jnp.repeat(jnp.exp(heights), extent[axis_at] // shards_of).reshape((-1,) + (1,) * (len(extent) - axis_at - 1))

    loudness = one(*shards[0])
    for cut in shards[1:]:
        loudness = loudness * one(*cut)
    return loudness


def noise(rng, extent, scale, limit, cuts=(), held_as=jnp.bfloat16):
    level = block_levels(rng, extent, cuts, -0.22, 0.18) if cuts else 1.0
    entries = jax.random.normal(rng, extent, jnp.float32) * scale * level
    return jnp.minimum(jnp.maximum(entries, -limit), limit).astype(held_as)


def setup_inputs(seed: int = 0) -> dict:
    streams_of = jax.random.split(jax.random.key(seed), 10)
    return {
        "state": noise(streams_of[0], (V, NX, NY), 1.0, 6.0, ((1, 8), (2, 16)), jnp.float32),
        "target": noise(streams_of[1], (V, NX, NY), 1.0, 6.0, ((1, 8), (2, 16))),
        "land_mask": touch_ends((jax.random.randint(streams_of[2], (NX, NY), 0, 2) < 1).astype(jnp.int32), jax.random.fold_in(streams_of[2], 1), 0, 1),
        "batch_map": touch_ends(jax.random.randint(streams_of[3], (NX, NY), 0, BATCHES), jax.random.fold_in(streams_of[3], 1), 0, BATCHES - 1).astype(jnp.int32),
        "diffusion": jnp.clip(jax.random.uniform(streams_of[4], (V,), jnp.float32, 0.05, 0.2), 0.05, 0.2),
        "speed_x": jnp.clip(jax.random.uniform(streams_of[5], (V,), jnp.float32, -0.3, 0.3), -0.3, 0.3),
        "speed_y": jnp.clip(jax.random.uniform(streams_of[6], (V,), jnp.float32, -0.3, 0.3), -0.3, 0.3),
        "w_in": noise(streams_of[7], (V, HID), V ** -0.5, 0.3125),
        "w_out": noise(streams_of[8], (HID, V), HID ** -0.5, 0.09375),
    }


def transport(field, diffusion, speed_x, speed_y):
    kap = diffusion[:, None, None]
    sxx = speed_x[:, None, None]
    syy = speed_y[:, None, None]
    padded = jnp.pad(field, ((0, 0), (1, 1), (1, 1)))
    centre = padded[:, 1:-1, 1:-1]
    east = padded[:, 2:, 1:-1]
    west = padded[:, :-2, 1:-1]
    north = padded[:, 1:-1, 2:]
    south = padded[:, 1:-1, :-2]
    return centre + kap * (east + west + north + south - 4.0 * centre) - 0.5 * sxx * (east - west) - 0.5 * syy * (north - south)


def reference(state, target, land_mask, batch_map, diffusion, speed_x, speed_y, w_in, w_out):
    field = state
    for substep in range(SUB):
        field = transport(field, diffusion, speed_x, speed_y)
    total = NX * NY
    inputs = field.reshape(V, total).T.astype(jnp.bfloat16)
    pre = jnp.dot(inputs, w_in, preferred_element_type=jnp.float32)
    hidden = jax.nn.silu(pre).astype(jnp.bfloat16)
    tend = jnp.dot(hidden, w_out, preferred_element_type=jnp.float32)
    weights = land_mask.reshape(total).astype(jnp.float32)[:, None]
    err = weights * (tend - target.reshape(V, total).T.astype(jnp.float32))
    new_state = field + 0.5 * (weights * tend).T.reshape(V, NX, NY)
    persq = 0.5 * jnp.sum(err * err, axis=1)
    onehot = (batch_map.reshape(total)[:, None] == jnp.arange(BATCHES, dtype=jnp.int32)[None, :]).astype(jnp.float32)
    batch_loss = jnp.dot(persq, onehot, precision=lax.Precision.HIGHEST) * (BATCHES / (total * V))
    dtend = (err * (total ** -0.5)).astype(jnp.bfloat16)
    dhid = jnp.dot(dtend, w_out.T, preferred_element_type=jnp.float32)
    sig = jax.nn.sigmoid(pre)
    dpre = (dhid * sig * (1.0 + pre * (1.0 - sig))).astype(jnp.bfloat16)
    grad_out = jnp.dot(hidden.T, dtend, preferred_element_type=jnp.float32)
    grad_in = jnp.dot(dpre.T, inputs, preferred_element_type=jnp.float32)
    return new_state, grad_in, grad_out, batch_loss
```

```python
import jax
import jax.numpy as jnp
from jax import lax
from jax.sharding import Mesh
from jax.sharding import PartitionSpec as P

SUB = 3
BATCHES = 64
BX = ("bx_0", "bx_1")
BY = ("by_0", "by_1", "by_2")
CORE = "by_2"
AXES = {"x": ("by_0", CORE), "y": ("bx_0", "by_1", CORE), "z": ("bx_1", CORE)}
ORDERS = ("xyz", "yzx", "zxy")
DIGITS = ((0, 3, 1, 2), (0, 1, 2, 3))
RING = {
    1: [(2 * p + c, 2 * (p ^ 1 if c == 0 else 3 - p) + c) for p in range(4) for c in range(2)],
    2: [(2 * p + c, 2 * (3 - p if c == 0 else p ^ 1) + c) for p in range(4) for c in range(2)],
}
PAIR = [(0, 1), (1, 0)]


def extended(cells, sides, width):
    for axis, dim in sides:
        count = lax.axis_size(axis)
        ends = count - 1
        head = lax.slice_in_dim(cells, 0, width, axis=dim)
        tail = lax.slice_in_dim(cells, cells.shape[dim] - width, cells.shape[dim], axis=dim)
        cells = jnp.concatenate(
            [
                lax.ppermute(tail, axis, [(i, (i + 1) % count) for i in range(ends)]),
                cells,
                lax.ppermute(head, axis, [((i + 1) % count, i) for i in range(ends)]),
            ],
            axis=dim,
        )
    return cells


def advance(padded, kap, sxx, syy):
    centre = padded[:, 1:-1, 1:-1]
    east = padded[:, 2:, 1:-1]
    west = padded[:, :-2, 1:-1]
    north = padded[:, 1:-1, 2:]
    south = padded[:, 1:-1, :-2]
    return (
        centre
        + kap * (east + west + north + south - 4.0 * centre)
        - 0.5 * sxx * (east - west)
        - 0.5 * syy * (north - south)
    )


def position(axis):
    if axis == "y":
        return lax.axis_index("bx_0") * 2 + lax.axis_index("by_1")
    return lax.axis_index("by_0" if axis == "x" else "bx_1")


def ring_places():
    core = lax.axis_index(CORE)
    places = {}
    for axis in "xyz":
        at = position(axis)
        folded = jnp.where(at == 0, 0, jnp.where(at == 3, 1, at + 1))
        places[axis] = jnp.where(core == 0, folded, at)
    return places


def half_of(rows, bit):
    size = rows.shape[0] // 2
    return lax.dynamic_slice_in_dim(rows, bit * size, size, 0)


def scatter_sums(kept, sent, places):
    received = lax.ppermute(sent, CORE, PAIR)
    done = []
    rows = kept.shape[0] // len(ORDERS)
    for stream, order in enumerate(ORDERS):
        mine = kept[stream * rows : (stream + 1) * rows] + received[stream * rows : (stream + 1) * rows]
        for axis in order:
            for turn in (1, 2):
                bit = places[axis] // 2 if turn == 1 else places[axis] % 2
                coming = lax.ppermute(half_of(mine, 1 - bit), AXES[axis], RING[turn])
                mine = half_of(mine, bit) + coming
        done.append(mine)
    return jnp.concatenate(done, axis=1)


def over_all(value):
    value = value + lax.ppermute(value, CORE, PAIR)
    for axis in "xyz":
        for turn in (1, 2):
            value = value + lax.ppermute(value, AXES[axis], RING[turn])
    return value


def in_ring_order(grad):
    split = grad.reshape(2, 4, 4, 2, 2, 32, 3, 128)
    cores = []
    for core in range(2):
        streams = []
        for stream, order in enumerate(ORDERS):
            part = split[:, :, :, :, core, :, stream].transpose(2, 0, 3, 1, 4, 5).reshape(4, 4, 4, 32, 128)
            part = part.transpose(*["xyz".index(axis) for axis in order], 3, 4)
            for dim in range(3):
                part = jnp.concatenate([lax.slice_in_dim(part, d, d + 1, axis=dim) for d in DIGITS[core]], axis=dim)
            streams.append(part.reshape(2048, 128))
        cores.append(jnp.concatenate(streams, axis=0))
    core = lax.axis_index(CORE)
    both = jnp.stack(cores)
    return lax.dynamic_index_in_dim(both, core, 0, False), lax.dynamic_index_in_dim(both, 1 - core, 0, False)


def on_device(state, target, land_mask, batch_map, diffusion, speed_x, speed_y, w_in, w_out):
    feats, rows_x, rows_y = state.shape
    kap = diffusion[:, None, None]
    sxx = speed_x[:, None, None]
    syy = speed_y[:, None, None]
    field = extended(state, ((BX, 1), (BY, 2)), SUB)
    for substep in range(SUB):
        field = advance(field, kap, sxx, syy)
        margin = SUB - substep - 1
        if margin > 0:
            along_x = (
                lax.axis_index(BX) * rows_x
                + jnp.arange(rows_x + 2 * margin, dtype=jnp.int32)
                - margin
            )
            along_y = (
                lax.axis_index(BY) * rows_y
                + jnp.arange(rows_y + 2 * margin, dtype=jnp.int32)
                - margin
            )
            inside_x = ((along_x >= 0) & (along_x < rows_x * lax.axis_size(BX))).astype(jnp.float32)
            inside_y = ((along_y >= 0) & (along_y < rows_y * lax.axis_size(BY))).astype(jnp.float32)
            field = field * inside_x[None, :, None] * inside_y[None, None, :]
    local_cols = rows_x * rows_y
    total = local_cols * lax.axis_size(BX) * lax.axis_size(BY)
    inputs = field.reshape(feats, local_cols).T.astype(jnp.bfloat16)
    pre = jnp.dot(inputs, w_in, preferred_element_type=jnp.float32)
    hidden = jax.nn.silu(pre).astype(jnp.bfloat16)
    tend = jnp.dot(hidden, w_out, preferred_element_type=jnp.float32)
    weights = land_mask.reshape(local_cols).astype(jnp.float32)[:, None]
    err = weights * (tend - target.reshape(feats, local_cols).T.astype(jnp.float32))
    new_state = field + 0.5 * (weights * tend).T.reshape(feats, rows_x, rows_y)
    persq = 0.5 * jnp.sum(err * err, axis=1)
    onehot = (
        batch_map.reshape(local_cols)[:, None] == jnp.arange(BATCHES, dtype=jnp.int32)[None, :]
    ).astype(jnp.float32)
    partial_loss = jnp.dot(persq, onehot, precision=lax.Precision.HIGHEST) * (
        BATCHES / (total * feats)
    )
    batch_loss = over_all(partial_loss)
    dtend = (err * total ** (-0.5)).astype(jnp.bfloat16)
    places = ring_places()
    grad_out = scatter_sums(
        *in_ring_order(jnp.dot(hidden.T, dtend, preferred_element_type=jnp.float32)), places
    )
    dhid = jnp.dot(dtend, w_out.T, preferred_element_type=jnp.float32)
    sig = jax.nn.sigmoid(pre)
    dpre = (dhid * sig * (1.0 + pre * (1.0 - sig))).astype(jnp.bfloat16)
    grad_in = scatter_sums(
        *in_ring_order(jnp.dot(dpre.T, inputs, preferred_element_type=jnp.float32)), places
    )
    return (new_state, grad_in, grad_out, batch_loss)


def solution(mesh):
    torus = Mesh(mesh.devices.reshape(2, 4, 4, 2, 2), BX + BY)
    return jax.shard_map(
        on_device,
        mesh=torus,
        in_specs=(P(None, BX, BY), P(None, BX, BY), P(BX, BY), P(BX, BY), P(), P(), P(), P(), P()),
        out_specs=(P(None, BX, BY), P(BX + BY, None), P(BX + BY, None), P()),
        check_vma=False,
    )
```

```python
import functools

import jax
import jax.numpy as jnp
import numpy as np
from jax import lax
from jax.experimental import pallas as pl
from jax.experimental.pallas import tpu as pltpu
from jax.sharding import Mesh
from jax.sharding import PartitionSpec as P

SUB = 3
BATCHES = 64
BX = ("bx_0", "bx_1")
BY = ("by_0", "by_1", "by_2")
CORE = "by_2"
AXES = {"x": ("by_0", CORE), "y": ("bx_0", "by_1", CORE), "z": ("bx_1", CORE)}
ORDERS = ("xyz", "yzx", "zxy")
DIGITS = ((0, 3, 1, 2), (0, 1, 2, 3))
RING = {
    1: [(2 * p + c, 2 * (p ^ 1 if c == 0 else 3 - p) + c) for p in range(4) for c in range(2)],
    2: [(2 * p + c, 2 * (3 - p if c == 0 else p ^ 1) + c) for p in range(4) for c in range(2)],
}
PAIR = [(0, 1), (1, 0)]


def extended(cells, sides, width):
    for axis, dim in sides:
        count = lax.axis_size(axis)
        ends = count - 1
        head = lax.slice_in_dim(cells, 0, width, axis=dim)
        tail = lax.slice_in_dim(cells, cells.shape[dim] - width, cells.shape[dim], axis=dim)
        cells = jnp.concatenate(
            [
                lax.ppermute(tail, axis, [(i, (i + 1) % count) for i in range(ends)]),
                cells,
                lax.ppermute(head, axis, [((i + 1) % count, i) for i in range(ends)]),
            ],
            axis=dim,
        )
    return cells


def advance(padded, kap, sxx, syy):
    centre = padded[:, 1:-1, 1:-1]
    east = padded[:, 2:, 1:-1]
    west = padded[:, :-2, 1:-1]
    north = padded[:, 1:-1, 2:]
    south = padded[:, 1:-1, :-2]
    return (
        centre
        + kap * (east + west + north + south - 4.0 * centre)
        - 0.5 * sxx * (east - west)
        - 0.5 * syy * (north - south)
    )


def position(axis):
    if axis == "y":
        return lax.axis_index("bx_0") * 2 + lax.axis_index("by_1")
    return lax.axis_index("by_0" if axis == "x" else "bx_1")


def ring_places():
    core = lax.axis_index(CORE)
    places = {}
    for axis in "xyz":
        at = position(axis)
        folded = jnp.where(at == 0, 0, jnp.where(at == 3, 1, at + 1))
        places[axis] = jnp.where(core == 0, folded, at)
    return places


def half_of(rows, bit):
    size = rows.shape[0] // 2
    return lax.dynamic_slice_in_dim(rows, bit * size, size, 0)


def ring_bits(places, axis):
    return (places[axis] // 2, places[axis] % 2)


def along_axis(mine, axis, places, riding=None):
    for turn, bit in enumerate(ring_bits(places, axis)):
        size = mine.shape[0] // 2
        leaving = half_of(mine, 1 - bit)
        if riding is not None:
            leaving = jnp.concatenate([leaving, riding], axis=0)
        coming = lax.ppermute(leaving, AXES[axis], RING[turn + 1])
        mine = half_of(mine, bit) + coming[:size]
        if riding is not None:
            riding = riding + coming[size:]
    return mine, riding


def scatter_sums(first, second, tile, places):
    from_core = [lax.ppermute(sent, CORE, PAIR) for _, sent in (first, second)]
    rows = first[0].shape[0] // len(ORDERS)
    riding = tile + from_core[0][first[0].shape[0] :]
    parts = []
    for (kept, _), received in zip((first, second), from_core):
        streams = []
        for stream, order in enumerate(ORDERS):
            at = slice(stream * rows, (stream + 1) * rows)
            carries = stream == 0 and kept is first[0]
            mine, carried = along_axis(
                kept[at] + received[at], order[0], places, riding if carries else None
            )
            riding = carried if carries else riding
            streams.append(mine)
        parts.append(streams)
    done = []
    riding = jnp.concatenate([riding, riding], axis=1)
    for stream, order in enumerate(ORDERS):
        mine = jnp.concatenate([parts[0][stream], parts[1][stream]], axis=1)
        for axis in order[1:]:
            mine, carried = along_axis(mine, axis, places, riding if stream == 0 else None)
            riding = carried if stream == 0 else riding
        done.append(mine)
    width = parts[0][0].shape[1]
    return (
        jnp.concatenate([d[:, :width] for d in done], axis=1),
        jnp.concatenate([d[:, width:] for d in done], axis=1),
        riding,
    )


def ring_rows():
    table = np.zeros((2, len(ORDERS), 64), np.int32)
    for core in range(2):
        for block in range(64):
            y_hi, z, x, y_lo = block // 32, block // 8 % 4, block // 2 % 4, block % 2
            at = {"x": x, "y": 2 * y_hi + y_lo, "z": z}
            for stream, order in enumerate(ORDERS):
                spot = 0
                for axis in order:
                    spot = spot * 4 + DIGITS[core].index(at[axis])
                table[core, stream, block] = (stream * 64 + spot) * 32
    return table.reshape(-1)


def put_rows(core_ref, table_ref, source_ref, base, right, kept_ref, sent_ref):
    core = core_ref[0]
    for slot, out_ref in enumerate((kept_ref, sent_ref)):
        digit = core if slot == 0 else 1 - core
        left = source_ref[:, digit].reshape(256, source_ref.shape[-1])
        sums = jnp.dot(left, right, preferred_element_type=jnp.float32)
        for block in range(8):
            for stream in range(3):
                row = table_ref[digit * 192 + stream * 64 + base + block]
                out_ref[pl.ds(pl.multiple_of(row, 32), 32), :] = sums[
                    block * 32 : (block + 1) * 32, stream * 128 : (stream + 1) * 128
                ]


def forward_kernel(
    scale, core_ref, table_ref, x_ref, win_ref, wout_t_ref, target_ref, mask_ref, batch_ref, field_ref,
    new_ref, slope_ref, dtend_ref, kept_ref, sent_ref, loss_ref, hidden_ref, tend_ref, right_ref,
):
    step = pl.program_id(0)

    @pl.when(step == 0)
    def _():
        tend_ref[...] = jnp.zeros_like(tend_ref)

    for part in range(2):
        rows = slice(part * 256, (part + 1) * 256)
        pre = jnp.dot(win_ref[rows, :], x_ref[...], preferred_element_type=jnp.float32)
        sig = 0.5 * jnp.tanh(0.5 * pre) + 0.5
        act = pre * sig
        slope_ref[rows, :] = sig + act * (1.0 - sig)
        hid = act.astype(jnp.bfloat16)
        hidden_ref[pl.ds(step * 8 + part * 4, 4)] = hid.reshape(4, 2, 32, hid.shape[-1])
        tend_ref[...] += jnp.dot(wout_t_ref[:, rows], hid, preferred_element_type=jnp.float32)

    @pl.when(step == pl.num_programs(0) - 1)
    def _():
        tend = tend_ref[...]
        mask = mask_ref[...].astype(jnp.float32)
        err = mask * (tend - target_ref[...].astype(jnp.float32))
        new_ref[...] = field_ref[...] + 0.5 * (mask * tend)
        persq = 0.5 * jnp.sum(err * err, axis=0, keepdims=True)
        batch = lax.broadcasted_iota(jnp.int32, (128, persq.shape[1]), 0)
        onehot = (batch == batch_ref[...]).astype(jnp.float32)
        loss = lax.dot_general(
            jnp.broadcast_to(persq, (8, persq.shape[1])),
            onehot,
            (((1,), (1,)), ((), ())),
            precision=lax.Precision.HIGHEST,
            preferred_element_type=jnp.float32,
        ) * scale[0]
        loss_ref[...] = loss
        sent_ref[pl.ds(kept_ref.shape[0], 8), :] = loss
        dtend = (err * scale[1]).astype(jnp.bfloat16)
        dtend_ref[...] = dtend
        right_ref[...] = dtend.T

        @pl.loop(0, 8)
        def _(piece):
            put_rows(
                core_ref, table_ref, hidden_ref.at[pl.ds(piece * 8, 8)], piece * 8, right_ref[...], kept_ref, sent_ref
            )


def backward_kernel(core_ref, table_ref, x_ref, wout_ref, slope_ref, dtend_ref, kept_ref, sent_ref, dpre_ref, right_ref):
    step = pl.program_id(0)

    @pl.when(step == 0)
    def _():
        right_ref[...] = x_ref[...].T

    for part in range(2):
        rows = slice(part * 256, (part + 1) * 256)
        dhid = jnp.dot(wout_ref[rows, :], dtend_ref[...], preferred_element_type=jnp.float32)
        dpre = (dhid * slope_ref[rows, :]).astype(jnp.bfloat16)
        dpre_ref[part * 4 : (part + 1) * 4] = dpre.reshape(4, 2, 32, dpre.shape[-1])
    put_rows(core_ref, table_ref, dpre_ref, step * 8, right_ref[...], kept_ref, sent_ref)


def whole(shape):
    return pl.BlockSpec(shape, lambda i, *_: (0,) * len(shape))


def network(x, field, target, mask, batch, w_in_t, w_out, total):
    feats, cols = x.shape
    hid = w_out.shape[0]
    core = lax.axis_index(CORE).astype(jnp.int32).reshape(1)
    table = jnp.asarray(ring_rows())
    rows = 3 * 2048
    f32, bf16 = jnp.float32, jnp.bfloat16
    new, slope, dtend, kept, sent, tile = pl.pallas_call(
        functools.partial(forward_kernel, (BATCHES / (total * feats), total ** (-0.5))),
        grid_spec=pltpu.PrefetchScalarGridSpec(
            num_scalar_prefetch=2,
            grid=(8,),
            in_specs=[
                whole((feats, cols)),
                pl.BlockSpec((512, feats), lambda i, *_: (i, 0)),
                pl.BlockSpec((feats, 512), lambda i, *_: (0, i)),
                whole((feats, cols)),
                whole((1, cols)),
                whole((1, cols)),
                whole((feats, cols)),
            ],
            out_specs=[
                whole((feats, cols)),
                pl.BlockSpec((512, cols), lambda i, *_: (i, 0)),
                whole((feats, cols)),
                whole((rows, 128)),
                whole((rows + 8, 128)),
                whole((8, 128)),
            ],
            scratch_shapes=[
                pltpu.VMEM((64, 2, 32, cols), bf16),
                pltpu.VMEM((feats, cols), f32),
                pltpu.VMEM((cols, feats), bf16),
            ],
        ),
        out_shape=[
            jax.ShapeDtypeStruct((feats, cols), f32),
            jax.ShapeDtypeStruct((hid, cols), f32),
            jax.ShapeDtypeStruct((feats, cols), bf16),
            jax.ShapeDtypeStruct((rows, 128), f32),
            jax.ShapeDtypeStruct((rows + 8, 128), f32),
            jax.ShapeDtypeStruct((8, 128), f32),
        ],
        compiler_params=pltpu.CompilerParams(
            dimension_semantics=("arbitrary",), vmem_limit_bytes=56 * 2**20
        ),
        cost_estimate=pl.CostEstimate(flops=6 * cols * feats * hid, bytes_accessed=30 * 2**20, transcendentals=cols * hid),
        name="forward",
    )(core, table, x, w_in_t, w_out.T, target, mask, batch, field)
    kept_in, sent_in = pl.pallas_call(
        backward_kernel,
        grid_spec=pltpu.PrefetchScalarGridSpec(
            num_scalar_prefetch=2,
            grid=(8,),
            in_specs=[
                whole((feats, cols)),
                pl.BlockSpec((512, feats), lambda i, *_: (i, 0)),
                pl.BlockSpec((512, cols), lambda i, *_: (i, 0)),
                whole((feats, cols)),
            ],
            out_specs=[whole((rows, 128)), whole((rows, 128))],
            scratch_shapes=[
                pltpu.VMEM((8, 2, 32, cols), bf16),
                pltpu.VMEM((cols, feats), bf16),
            ],
        ),
        out_shape=[jax.ShapeDtypeStruct((rows, 128), f32), jax.ShapeDtypeStruct((rows, 128), f32)],
        compiler_params=pltpu.CompilerParams(
            dimension_semantics=("arbitrary",), vmem_limit_bytes=32 * 2**20
        ),
        cost_estimate=pl.CostEstimate(flops=4 * cols * feats * hid, bytes_accessed=28 * 2**20, transcendentals=0),
        name="backward",
    )(core, table, x, w_out, slope, dtend)
    return new, (kept, sent), (kept_in, sent_in), tile


def on_device(state, target, land_mask, batch_map, diffusion, speed_x, speed_y, w_in, w_out):
    feats, rows_x, rows_y = state.shape
    kap = diffusion[:, None, None]
    sxx = speed_x[:, None, None]
    syy = speed_y[:, None, None]
    field = extended(state, ((BX, 1), (BY, 2)), SUB)
    for substep in range(SUB):
        field = advance(field, kap, sxx, syy)
        margin = SUB - substep - 1
        if margin > 0:
            along_x = (
                lax.axis_index(BX) * rows_x
                + jnp.arange(rows_x + 2 * margin, dtype=jnp.int32)
                - margin
            )
            along_y = (
                lax.axis_index(BY) * rows_y
                + jnp.arange(rows_y + 2 * margin, dtype=jnp.int32)
                - margin
            )
            inside_x = ((along_x >= 0) & (along_x < rows_x * lax.axis_size(BX))).astype(jnp.float32)
            inside_y = ((along_y >= 0) & (along_y < rows_y * lax.axis_size(BY))).astype(jnp.float32)
            field = field * inside_x[None, :, None] * inside_y[None, None, :]
    local_cols = rows_x * rows_y
    total = local_cols * lax.axis_size(BX) * lax.axis_size(BY)
    flat = field.reshape(feats, local_cols)
    new, first, second, tile = network(
        flat.astype(jnp.bfloat16),
        flat,
        target.reshape(feats, local_cols),
        land_mask.reshape(1, local_cols),
        batch_map.reshape(1, local_cols),
        w_in.T,
        w_out,
        total,
    )
    grad_out, grad_in, losses = scatter_sums(first, second, tile, ring_places())
    return (new.reshape(feats, rows_x, rows_y), grad_in, grad_out, losses[0, :BATCHES])


def solution(mesh):
    torus = Mesh(mesh.devices.reshape(2, 4, 4, 2, 2), BX + BY)
    return jax.shard_map(
        on_device,
        mesh=torus,
        in_specs=(P(None, BX, BY), P(None, BX, BY), P(BX, BY), P(BX, BY), P(), P(), P(), P(), P()),
        out_specs=(P(None, BX, BY), P(BX + BY, None), P(BX + BY, None), P()),
        check_vma=False,
    )
```

```python
import functools

import jax
import jax.numpy as jnp
import numpy as np
from jax import lax
from jax.experimental import pallas as pl
from jax.experimental.pallas import tpu as pltpu
from jax.sharding import Mesh
from jax.sharding import PartitionSpec as P

SUB = 3
BATCHES = 64
FEW = 640
BX = ("bx_0", "bx_1")
BY = ("by_0", "by_1", "by_2")
CORE = "by_2"
AXES = {"x": ("by_0", CORE), "y": ("bx_0", "by_1", CORE), "z": ("bx_1", CORE)}
ORDERS = ("xyz", "yzx", "zxy")
DIGITS = ((0, 3, 1, 2), (0, 1, 2, 3))
RING = {
    1: [(2 * p + c, 2 * (p ^ 1 if c == 0 else 3 - p) + c) for p in range(4) for c in range(2)],
    2: [(2 * p + c, 2 * (3 - p if c == 0 else p ^ 1) + c) for p in range(4) for c in range(2)],
}
PAIR = [(0, 1), (1, 0)]


def extended(cells, sides, width):
    for axis, dim in sides:
        count = lax.axis_size(axis)
        ends = count - 1
        head = lax.slice_in_dim(cells, 0, width, axis=dim)
        tail = lax.slice_in_dim(cells, cells.shape[dim] - width, cells.shape[dim], axis=dim)
        cells = jnp.concatenate(
            [
                lax.ppermute(tail, axis, [(i, (i + 1) % count) for i in range(ends)]),
                cells,
                lax.ppermute(head, axis, [((i + 1) % count, i) for i in range(ends)]),
            ],
            axis=dim,
        )
    return cells


def advance(padded, kap, sxx, syy):
    centre = padded[:, 1:-1, 1:-1]
    east = padded[:, 2:, 1:-1]
    west = padded[:, :-2, 1:-1]
    north = padded[:, 1:-1, 2:]
    south = padded[:, 1:-1, :-2]
    return (
        centre
        + kap * (east + west + north + south - 4.0 * centre)
        - 0.5 * sxx * (east - west)
        - 0.5 * syy * (north - south)
    )


def position(axis):
    if axis == "y":
        return lax.axis_index("bx_0") * 2 + lax.axis_index("by_1")
    return lax.axis_index("by_0" if axis == "x" else "bx_1")


def ring_places():
    core = lax.axis_index(CORE)
    places = {}
    for axis in "xyz":
        at = position(axis)
        folded = jnp.where(at == 0, 0, jnp.where(at == 3, 1, at + 1))
        places[axis] = jnp.where(core == 0, folded, at)
    return places


def half_of(rows, bit):
    size = rows.shape[0] // 2
    return lax.dynamic_slice_in_dim(rows, bit * size, size, 0)


def ring_bits(places, axis):
    return (places[axis] // 2, places[axis] % 2)


def ring_turn(mine, axis, turn, places, riding=None):
    bit = places[axis] % 2 if turn else places[axis] // 2
    size = mine.shape[0] // 2
    leaving = half_of(mine, 1 - bit)
    if riding is not None:
        leaving = jnp.concatenate([leaving, riding], axis=0)
    coming = lax.ppermute(leaving, AXES[axis], RING[turn + 1])
    mine = half_of(mine, bit) + coming[:size]
    return mine, (None if riding is None else riding + coming[size:])


def ring_round(streams, stage, turn, places, riding=None):
    moved = []
    for stream, order in enumerate(ORDERS):
        mine, carried = ring_turn(
            streams[stream], order[stage], turn, places, riding if stream == 0 else None
        )
        riding = carried if stream == 0 else riding
        moved.append(mine)
    return moved, riding


def core_sums(kept, received):
    rows = kept.shape[0] // len(ORDERS)
    return [
        kept[stream * rows : (stream + 1) * rows] + received[stream * rows : (stream + 1) * rows]
        for stream in range(len(ORDERS))
    ]


def ring_rows():
    table = np.zeros((2, len(ORDERS), 64), np.int32)
    for core in range(2):
        for block in range(64):
            y_hi, z, x, y_lo = block // 32, block // 8 % 4, block // 2 % 4, block % 2
            at = {"x": x, "y": 2 * y_hi + y_lo, "z": z}
            for stream, order in enumerate(ORDERS):
                spot = 0
                for axis in order:
                    spot = spot * 4 + DIGITS[core].index(at[axis])
                table[core, stream, block] = (stream * 64 + spot) * 32
    return table.reshape(-1)


def put_rows(scalar_ref, table_ref, source_ref, base, right, kept_ref, sent_ref):
    core = scalar_ref[0]
    for slot, out_ref in enumerate((kept_ref, sent_ref)):
        digit = core if slot == 0 else 1 - core
        left = source_ref[:, digit, :, : right.shape[0]].reshape(256, right.shape[0])
        sums = jnp.dot(left, right, preferred_element_type=jnp.float32)
        for block in range(8):
            for stream in range(3):
                row = table_ref[digit * 192 + stream * 64 + base + block]
                out_ref[pl.ds(pl.multiple_of(row, 32), 32), :] = sums[
                    block * 32 : (block + 1) * 32, stream * 128 : (stream + 1) * 128
                ]


def by_width(scalar_ref, most, body):
    land = scalar_ref[1]
    pl.when(land <= FEW)(functools.partial(body, FEW))
    pl.when(land > FEW)(functools.partial(body, most))


ROWS = (((1,), (1,)), ((), ()))


def forward_kernel(
    scale, scalar_ref, table_ref, x_ref, win_ref, wout_t_ref, target_ref, rank_ref, batch_ref, field_ref,
    new_ref, slope_ref, dtend_ref, xn_ref, kept_ref, sent_ref, hidden_ref, tend_ref, right_ref, pick_ref, xc_ref,
):
    step = pl.program_id(0)
    cols = x_ref.shape[1]

    def start(n):
        for at in range(0, n, 128):
            slot = lax.broadcasted_iota(jnp.int32, (128, cols), 0) + at
            pick_ref[at : at + 128, :] = jnp.where(slot == rank_ref[...], 1.0, 0.0).astype(jnp.bfloat16)
        packed = lax.dot_general(x_ref[...], pick_ref[:n, :], ROWS, preferred_element_type=jnp.float32)
        packed = packed.astype(jnp.bfloat16)
        xc_ref[:, :n] = packed
        xn_ref[:n, :] = packed.T
        tend_ref[:, :n] = jnp.zeros((tend_ref.shape[0], n), jnp.float32)

    def run(n):
        for part in range(2):
            rows = slice(part * 256, (part + 1) * 256)
            pre = jnp.dot(win_ref[rows, :], xc_ref[:, :n], preferred_element_type=jnp.float32)
            sig = 0.5 * jnp.tanh(0.5 * pre) + 0.5
            act = pre * sig
            slope_ref[rows, :n] = sig + act * (1.0 - sig)
            hid = act.astype(jnp.bfloat16)
            hidden_ref[pl.ds(step * 8 + part * 4, 4), :, :, :n] = hid.reshape(4, 2, 32, n)
            tend_ref[:, :n] += jnp.dot(wout_t_ref[:, rows], hid, preferred_element_type=jnp.float32)

    def finish(n):
        pick = pick_ref[:n, :]
        tend = tend_ref[:, :n]
        wanted = lax.dot_general(target_ref[...], pick, ROWS, preferred_element_type=jnp.float32)
        err = tend - wanted
        coarse = tend.astype(jnp.bfloat16)
        fine = (tend - coarse.astype(jnp.float32)).astype(jnp.bfloat16)
        spread = jnp.dot(coarse, pick, preferred_element_type=jnp.float32)
        spread += jnp.dot(fine, pick, preferred_element_type=jnp.float32)
        new_ref[...] = field_ref[...] + 0.5 * spread
        persq = 0.5 * jnp.sum(err * err, axis=0, keepdims=True)
        batch = lax.dot_general(batch_ref[...], pick, ROWS, preferred_element_type=jnp.float32)
        which = lax.broadcasted_iota(jnp.int32, (128, n), 0).astype(jnp.float32)
        onehot = jnp.where(which == batch[0:1, :], 1.0, 0.0)
        sent_ref[pl.ds(kept_ref.shape[0], 8), :] = scale[0] * lax.dot_general(
            jnp.broadcast_to(persq, (8, n)),
            onehot,
            ROWS,
            precision=lax.Precision.HIGHEST,
            preferred_element_type=jnp.float32,
        )
        dtend = (err * scale[1]).astype(jnp.bfloat16)
        dtend_ref[:, :n] = dtend
        right_ref[:n, :] = dtend.T

        @pl.loop(0, 8)
        def _(piece):
            put_rows(
                scalar_ref, table_ref, hidden_ref.at[pl.ds(piece * 8, 8)], piece * 8, right_ref[:n, :], kept_ref, sent_ref
            )

    pl.when(step == 0)(lambda: by_width(scalar_ref, cols, start))
    by_width(scalar_ref, cols, run)
    pl.when(step == pl.num_programs(0) - 1)(lambda: by_width(scalar_ref, cols, finish))


def dpre_kernel(scalar_ref, wout_ref, slope_ref, dtend_ref, dpre_ref):
    def run(n):
        for part in range(2):
            rows = slice(part * 256, (part + 1) * 256)
            dhid = jnp.dot(wout_ref[rows, :], dtend_ref[:, :n], preferred_element_type=jnp.float32)
            dpre = (dhid * slope_ref[rows, :n]).astype(jnp.bfloat16)
            dpre_ref[part * 4 : (part + 1) * 4, :, :, :n] = dpre.reshape(4, 2, 32, n)

    by_width(scalar_ref, dtend_ref.shape[1], run)


def grad_kernel(scalar_ref, table_ref, dpre_ref, xn_ref, kept_ref, sent_ref):
    base = pl.program_id(0) * 8

    def run(n):
        put_rows(scalar_ref, table_ref, dpre_ref, base, xn_ref[:n, :], kept_ref, sent_ref)

    by_width(scalar_ref, xn_ref.shape[0], run)


def whole(*shape):
    return pl.BlockSpec(shape, lambda i, *_: (0,) * len(shape))


def shaped(dtype, *shape):
    return jax.ShapeDtypeStruct(shape, dtype)


def params(megabytes):
    return pltpu.CompilerParams(dimension_semantics=("arbitrary",), vmem_limit_bytes=megabytes * 2**20)


def land_ranks(mask):
    rows, cols = mask.shape
    ones = mask.astype(jnp.float32)
    before = jnp.triu(jnp.ones((cols, cols), jnp.float32), 1)
    within = jnp.dot(ones, before)
    above = jnp.dot(jnp.tril(jnp.ones((rows, rows), jnp.float32), -1), jnp.sum(ones, axis=1, keepdims=True))
    ranks = jnp.where(mask > 0, (within + above).astype(jnp.int32), -1)
    return ranks.reshape(1, rows * cols), jnp.sum(mask).astype(jnp.int32)


def network(x, field, target, mask, batch, w_in_t, w_out, total, places):
    feats, cols = x.shape
    hid = w_out.shape[0]
    ranks, land = land_ranks(mask)
    scalars = jnp.stack([lax.axis_index(CORE).astype(jnp.int32), land])
    table = jnp.asarray(ring_rows())
    rows = len(ORDERS) * 2048
    f32, bf16 = jnp.float32, jnp.bfloat16
    cut = lambda *shape: pl.BlockSpec(shape, lambda i, *_: (i,) + (0,) * (len(shape) - 1))
    new, slope, dtend, xn, kept, sent = pl.pallas_call(
        functools.partial(forward_kernel, (BATCHES / (total * feats), total ** (-0.5))),
        grid_spec=pltpu.PrefetchScalarGridSpec(
            num_scalar_prefetch=2,
            grid=(8,),
            in_specs=[
                whole(feats, cols),
                cut(512, feats),
                pl.BlockSpec((feats, 512), lambda i, *_: (0, i)),
                whole(feats, cols),
                whole(1, cols),
                whole(8, cols),
                whole(feats, cols),
            ],
            out_specs=[
                whole(feats, cols),
                cut(512, cols),
                whole(feats, cols),
                whole(cols, feats),
                whole(rows, 128),
                whole(rows + 8, 128),
            ],
            scratch_shapes=[
                pltpu.VMEM((64, 2, 32, cols), bf16),
                pltpu.VMEM((feats, cols), f32),
                pltpu.VMEM((cols, feats), bf16),
                pltpu.VMEM((cols, cols), bf16),
                pltpu.VMEM((feats, cols), bf16),
            ],
        ),
        out_shape=[
            shaped(f32, feats, cols),
            shaped(f32, hid, cols),
            shaped(bf16, feats, cols),
            shaped(bf16, cols, feats),
            shaped(f32, rows, 128),
            shaped(f32, rows + 8, 128),
        ],
        compiler_params=params(56),
        cost_estimate=pl.CostEstimate(
            flops=4 * cols * feats * hid, bytes_accessed=40 * 2**20, transcendentals=cols * hid
        ),
        name="forward",
    )(scalars, table, x, w_in_t, w_out.T, target, ranks, batch, field)
    from_core = lax.ppermute(sent, CORE, PAIR)
    dpre = pl.pallas_call(
        dpre_kernel,
        grid_spec=pltpu.PrefetchScalarGridSpec(
            num_scalar_prefetch=1,
            grid=(8,),
            in_specs=[cut(512, feats), cut(512, cols), whole(feats, cols)],
            out_specs=cut(8, 2, 32, cols),
        ),
        out_shape=shaped(bf16, 64, 2, 32, cols),
        compiler_params=params(24),
        cost_estimate=pl.CostEstimate(flops=2 * cols * feats * hid, bytes_accessed=28 * 2**20, transcendentals=0),
        name="dpre",
    )(scalars, w_out, slope, dtend)
    dpre, from_core = lax.optimization_barrier((dpre, from_core))
    first = core_sums(kept, from_core[:rows])
    first, losses = ring_round(first, 0, 0, places, from_core[rows:] + sent[rows:])
    kept_in, sent_in = pl.pallas_call(
        grad_kernel,
        grid_spec=pltpu.PrefetchScalarGridSpec(
            num_scalar_prefetch=2,
            grid=(8,),
            in_specs=[cut(8, 2, 32, cols), whole(cols, feats)],
            out_specs=[whole(rows, 128), whole(rows, 128)],
        ),
        out_shape=[shaped(f32, rows, 128), shaped(f32, rows, 128)],
        compiler_params=params(24),
        cost_estimate=pl.CostEstimate(flops=2 * cols * feats * hid, bytes_accessed=14 * 2**20, transcendentals=0),
        name="grad",
    )(scalars, table, dpre, xn)
    kept_in, sent_in, *first, losses = lax.optimization_barrier((kept_in, sent_in, *first, losses))
    from_core = lax.ppermute(sent_in, CORE, PAIR)
    first, losses = ring_round(first, 0, 1, places, losses)
    second = core_sums(kept_in, from_core)
    for turn in range(2):
        second, _ = ring_round(second, 0, turn, places)
    both = [jnp.concatenate(pair, axis=1) for pair in zip(first, second)]
    losses = jnp.concatenate([losses, losses], axis=1)
    for stage in (1, 2):
        for turn in range(2):
            both, losses = ring_round(both, stage, turn, places, losses)
    grad_out = jnp.concatenate([b[:, :128] for b in both], axis=1)
    grad_in = jnp.concatenate([b[:, 128:] for b in both], axis=1)
    return new, grad_in, grad_out, losses[0, :BATCHES]


def on_device(state, target, land_mask, batch_map, diffusion, speed_x, speed_y, w_in, w_out):
    feats, rows_x, rows_y = state.shape
    kap = diffusion[:, None, None]
    sxx = speed_x[:, None, None]
    syy = speed_y[:, None, None]
    field = extended(state, ((BX, 1), (BY, 2)), SUB)
    for substep in range(SUB):
        field = advance(field, kap, sxx, syy)
        margin = SUB - substep - 1
        if margin > 0:
            along_x = (
                lax.axis_index(BX) * rows_x
                + jnp.arange(rows_x + 2 * margin, dtype=jnp.int32)
                - margin
            )
            along_y = (
                lax.axis_index(BY) * rows_y
                + jnp.arange(rows_y + 2 * margin, dtype=jnp.int32)
                - margin
            )
            inside_x = ((along_x >= 0) & (along_x < rows_x * lax.axis_size(BX))).astype(jnp.float32)
            inside_y = ((along_y >= 0) & (along_y < rows_y * lax.axis_size(BY))).astype(jnp.float32)
            field = field * inside_x[None, :, None] * inside_y[None, None, :]
    local_cols = rows_x * rows_y
    total = local_cols * lax.axis_size(BX) * lax.axis_size(BY)
    flat = field.reshape(feats, local_cols)
    new, grad_in, grad_out, batch_loss = network(
        flat.astype(jnp.bfloat16),
        flat,
        target.reshape(feats, local_cols),
        land_mask,
        jnp.broadcast_to(batch_map.reshape(1, local_cols), (8, local_cols)).astype(jnp.bfloat16),
        w_in.T,
        w_out,
        total,
        ring_places(),
    )
    return (new.reshape(feats, rows_x, rows_y), grad_in, grad_out, batch_loss)


def solution(mesh):
    torus = Mesh(mesh.devices.reshape(2, 4, 4, 2, 2), BX + BY)
    return jax.shard_map(
        on_device,
        mesh=torus,
        in_specs=(P(None, BX, BY), P(None, BX, BY), P(BX, BY), P(BX, BY), P(), P(), P(), P(), P()),
        out_specs=(P(None, BX, BY), P(BX + BY, None), P(BX + BY, None), P()),
        check_vma=False,
    )
```

```python
import functools

import jax
import jax.numpy as jnp
import numpy as np
from jax import lax
from jax.experimental import pallas as pl
from jax.experimental.pallas import tpu as pltpu
from jax.sharding import Mesh
from jax.sharding import PartitionSpec as P

SUB = 3
BATCHES = 64
FEW = 640
BX = ("bx_0", "bx_1")
BY = ("by_0", "by_1", "by_2")
CORE = "by_2"
AXES = {"x": ("by_0", CORE), "y": ("bx_0", "by_1", CORE), "z": ("bx_1", CORE)}
ORDERS = ("xyz", "yzx", "zxy")
DIGITS = ((0, 3, 1, 2), (0, 1, 2, 3))
RING = {
    1: [(2 * p + c, 2 * (p ^ 1 if c == 0 else 3 - p) + c) for p in range(4) for c in range(2)],
    2: [(2 * p + c, 2 * (3 - p if c == 0 else p ^ 1) + c) for p in range(4) for c in range(2)],
}
PAIR = [(0, 1), (1, 0)]


def edge_kernel(state_ref, low_ref, high_ref, left_ref, right_ref):
    for row in range(8):
        cells = state_ref[pl.ds(row, 128, stride=8), :]
        if row < SUB:
            low_ref[0, row * 128 : (row + 1) * 128, :] = cells
        if row >= 8 - SUB:
            high_ref[0, (row - 8 + SUB) * 128 : (row - 7 + SUB) * 128, :] = cells
        turned = cells.T
        left_ref[0, row * 8 : (row + 1) * 8, :] = turned[:8, :]
        right_ref[0, row * 8 : (row + 1) * 8, :] = turned[120:, :]


def transport_kernel(
    state_ref, above_ref, below_ref, left_ref, right_ref,
    coef_0, coef_1, coef_2, coef_3, coef_4, field_ref, x_ref, even_ref, odd_ref,
):
    lane = lax.broadcasted_iota(jnp.int32, (128, 128), 1)
    gap = jnp.zeros((112, 128), jnp.float32)
    at_x, at_y = lax.axis_index(BX), lax.axis_index(BY)
    inside = [jnp.where(at_x > 0, 1.0, 0.0), jnp.where(at_x < lax.axis_size(BX) - 1, 1.0, 0.0)]
    beside = jnp.where(
        lane < 64, jnp.where(at_y < lax.axis_size(BY) - 1, 1.0, 0.0), jnp.where(at_y > 0, 1.0, 0.0)
    )
    for row in range(-SUB, 8 + SUB):
        if 0 <= row < 8:
            cells = state_ref[pl.ds(row, 128, stride=8), :]
            left, right = (ref[0, row * 8 : (row + 1) * 8, :] for ref in (left_ref, right_ref))
        else:
            far_ref, at = (above_ref, row + SUB) if row < 0 else (below_ref, row - 8)
            cells = far_ref[0, at * 128 : (at + 1) * 128, :]
            left, right = (
                far_ref[0, side + at * 8 : side + (at + 1) * 8, :]
                for side in (SUB * 128, SUB * 136)
            )
        even_ref[row + SUB, 0] = cells
        even_ref[row + SUB, 1] = jnp.concatenate([right, gap, left], axis=0).T
    here, there = even_ref, odd_ref
    for substep in range(SUB):
        margin = SUB - substep - 1
        for row in range(-margin, 8 + margin):
            at = row + SUB
            main, side = here[at, 0], here[at, 1]
            main_up, side_up = pltpu.roll(main, 127, 1), pltpu.roll(side, 127, 1)
            main_down, side_down = pltpu.roll(main, 1, 1), pltpu.roll(side, 1, 1)
            new = (
                coef_0[...] * main
                + coef_1[...] * here[at + 1, 0]
                + coef_2[...] * here[at - 1, 0]
                + coef_3[...] * jnp.where(lane == 127, side_up, main_up)
                + coef_4[...] * jnp.where(lane == 0, side_down, main_down)
            )
            if margin == 0:
                field_ref[:, row * 128 : (row + 1) * 128] = new
                x_ref[:, row * 128 : (row + 1) * 128] = new.astype(jnp.bfloat16)
                continue
            near = (
                coef_0[...] * side
                + coef_1[...] * here[at + 1, 1]
                + coef_2[...] * here[at - 1, 1]
                + coef_3[...] * jnp.where(lane == 127, main_up, side_up)
                + coef_4[...] * jnp.where(lane == 0, main_down, side_down)
            ) * beside
            if row < 0 or row > 7:
                new = new * inside[0 if row < 0 else 1]
                near = near * inside[0 if row < 0 else 1]
            there[at, 0] = new
            there[at, 1] = near
        here, there = there, here


def shifted(value, axis, step):
    count = lax.axis_size(axis)
    pairs = [(i, i + step) for i in range(count) if 0 <= i + step < count]
    return lax.ppermute(value, axis, pairs)


def transported(state, diffusion, speed_x, speed_y):
    feats = state.shape[0]
    f32 = jnp.float32
    flat = in_hbm(state.reshape(feats * 8, 128))
    chunk = lambda rows: pl.BlockSpec((1, rows, 128), lambda i: (i, 0, 0))
    low, high, left, right = pl.pallas_call(
        edge_kernel,
        grid=(feats // 128,),
        in_specs=[pl.BlockSpec((1024, 128), lambda i: (i, 0))],
        out_specs=[chunk(SUB * 144), chunk(SUB * 144), chunk(64), chunk(64)],
        out_shape=[shaped(f32, feats // 128, rows, 128) for rows in (SUB * 144, SUB * 144, 64, 64)],
        compiler_params=params(16),
        cost_estimate=pl.CostEstimate(flops=2**20, bytes_accessed=3 * 2**20, transcendentals=0),
        name="edges",
    )(flat)
    from_left = shifted(right, BY, 1)
    from_right = shifted(left, BY, -1)
    low, high = (
        lax.dynamic_update_slice(
            edge, jnp.concatenate([from_left[:, rows], from_right[:, rows]], axis=1), (0, SUB * 128, 0)
        )
        for edge, rows in ((low, slice(0, SUB * 8)), (high, slice((8 - SUB) * 8, 64)))
    )
    above = shifted(high, BX, 1)
    below = shifted(low, BX, -1)
    coefs = [
        jnp.broadcast_to(value[:, None], (feats, 128))
        for value in (
            1.0 - 4.0 * diffusion,
            diffusion - 0.5 * speed_x,
            diffusion + 0.5 * speed_x,
            diffusion - 0.5 * speed_y,
            diffusion + 0.5 * speed_y,
        )
    ]
    field, x = pl.pallas_call(
        transport_kernel,
        grid=(feats // 128,),
        in_specs=[
            pl.BlockSpec((1024, 128), lambda i: (i, 0)),
            chunk(SUB * 144),
            chunk(SUB * 144),
            chunk(64),
            chunk(64),
        ]
        + [pl.BlockSpec((128, 128), lambda i: (i, 0))] * 5,
        out_specs=[pl.BlockSpec((128, 1024), lambda i: (i, 0))] * 2,
        scratch_shapes=[pltpu.VMEM((14, 2, 128, 128), f32)] * 2,
        out_shape=[pltpu.HBM((feats, 1024), f32), pltpu.HBM((feats, 1024), jnp.bfloat16)],
        compiler_params=params(16),
        cost_estimate=pl.CostEstimate(flops=2**24, bytes_accessed=6 * 2**20, transcendentals=0),
        name="transport",
    )(flat, above, below, from_left, from_right, *coefs)
    return field, x, (from_left, from_right)


def position(axis):
    if axis == "y":
        return lax.axis_index("bx_0") * 2 + lax.axis_index("by_1")
    return lax.axis_index("by_0" if axis == "x" else "bx_1")


def ring_places():
    core = lax.axis_index(CORE)
    places = {}
    for axis in "xyz":
        at = position(axis)
        folded = jnp.where(at == 0, 0, jnp.where(at == 3, 1, at + 1))
        places[axis] = jnp.where(core == 0, folded, at)
    return places


def half_of(rows, size, bit):
    return lax.dynamic_slice_in_dim(rows, bit * size, size, 0)


def ring_turn(terms, axis, turn, places, riding=None):
    bit = places[axis] % 2 if turn else places[axis] // 2
    size = terms[0].shape[0] // 2
    leaving = sum(half_of(term, size, 1 - bit) for term in terms)
    if riding is not None:
        leaving = jnp.concatenate([leaving, riding], axis=0)
    coming = lax.ppermute(leaving, AXES[axis], RING[turn + 1])
    staying = sum(half_of(term, size, bit) for term in terms)
    return [staying + coming[:size]], (None if riding is None else riding + coming[size:])


def ring_round(streams, stage, turn, places, riding=None):
    moved = []
    for stream, order in enumerate(ORDERS):
        terms, carried = ring_turn(
            streams[stream], order[stage], turn, places, riding if stream == 0 else None
        )
        riding = carried if stream == 0 else riding
        moved.append(terms)
    return moved, riding


def ring_rows():
    table = np.zeros((2, len(ORDERS), 64), np.int32)
    for core in range(2):
        for block in range(64):
            y_hi, z, x, y_lo = block // 32, block // 8 % 4, block // 2 % 4, block % 2
            at = {"x": x, "y": 2 * y_hi + y_lo, "z": z}
            for stream, order in enumerate(ORDERS):
                spot = 0
                for axis in order:
                    spot = spot * 4 + DIGITS[core].index(at[axis])
                table[core, stream, block] = spot * 32
    return table.reshape(-1)


def put_rows(table_ref, source_ref, base, right, lanes, kept_refs, sent_refs):
    core = lax.axis_index(CORE)
    for slot, out_refs in enumerate((kept_refs, sent_refs)):
        digit = core if slot == 0 else 1 - core
        left = source_ref[:, digit, :, : right.shape[0]].reshape(256, right.shape[0])
        sums = jnp.dot(left, right, preferred_element_type=jnp.float32)
        for block in range(8):
            for stream in range(3):
                row = table_ref[digit * 192 + stream * 64 + base + block]
                out_refs[stream][pl.ds(pl.multiple_of(row, 32), 32), lanes] = sums[
                    block * 32 : (block + 1) * 32, stream * 128 : (stream + 1) * 128
                ]


def by_width(scalar_ref, most, body):
    land = scalar_ref[0]
    pl.when(land <= FEW)(functools.partial(body, FEW))
    pl.when(land > FEW)(functools.partial(body, most))


ROWS = (((1,), (1,)), ((), ()))


def network_kernel(
    scale, scalar_ref, table_ref, x_ref, win_ref, wout_f_ref, wout_ref, target_ref, rank_ref, batch_ref, field_ref,
    new_ref, kept_a, kept_b, kept_c, sent_a, sent_b, sent_c, loss_ref,
    slope_ref, hidden_ref, tend_ref, pick_ref, xc_ref, xn_ref, dtend_ref, dtn_ref, dpre_ref,
):
    step = pl.program_id(0)
    feats, cols = x_ref.shape
    kept, sent = (kept_a, kept_b, kept_c), (sent_a, sent_b, sent_c)

    def start(n):
        for at in range(0, n, 128):
            slot = lax.broadcasted_iota(jnp.int32, (128, cols), 0) + at
            pick_ref[at : at + 128, :] = jnp.where(slot == rank_ref[...], 1.0, 0.0).astype(jnp.bfloat16)
        packed = lax.dot_general(x_ref[...], pick_ref[:n, :], ROWS, preferred_element_type=jnp.float32)
        packed = packed.astype(jnp.bfloat16)
        xc_ref[:, :n] = packed
        xn_ref[:n, :] = packed.T
        tend_ref[:, :n] = jnp.zeros((feats, n), jnp.float32)

    def forward(n):
        for part in range(2):
            rows = slice(part * 256, (part + 1) * 256)
            pre = jnp.dot(win_ref[:, rows].T, xc_ref[:, :n], preferred_element_type=jnp.float32)
            sig = 0.5 * jnp.tanh(0.5 * pre) + 0.5
            act = pre * sig
            slope_ref[pl.ds(pl.multiple_of(step * 512 + part * 256, 256), 256), :n] = sig + act * (1.0 - sig)
            hid = act.astype(jnp.bfloat16)
            hidden_ref[pl.ds(step * 8 + part * 4, 4), :, :, :n] = hid.reshape(4, 2, 32, n)
            tend_ref[:, :n] += jnp.dot(wout_f_ref[rows, :].T, hid, preferred_element_type=jnp.float32)

    def middle(n):
        pick = pick_ref[:n, :]
        tend = tend_ref[:, :n]
        wanted = lax.dot_general(target_ref[...], pick, ROWS, preferred_element_type=jnp.float32)
        err = tend - wanted
        dtend = (err * scale[1]).astype(jnp.bfloat16)
        dtend_ref[:, :n] = dtend
        dtn_ref[:n, :] = dtend.T
        coarse = tend.astype(jnp.bfloat16)
        fine = (tend - coarse.astype(jnp.float32)).astype(jnp.bfloat16)
        spread = jnp.dot(coarse, pick, preferred_element_type=jnp.float32)
        spread += jnp.dot(fine, pick, preferred_element_type=jnp.float32)
        new = field_ref[...] + 0.5 * spread
        for row in range(8):
            new_ref[pl.ds(row, feats, stride=8), :] = new[:, row * 128 : (row + 1) * 128]
        persq = 0.5 * jnp.sum(err * err, axis=0, keepdims=True)
        batch = lax.dot_general(batch_ref[...], pick, ROWS, preferred_element_type=jnp.float32)
        which = lax.broadcasted_iota(jnp.int32, (128, n), 0).astype(jnp.float32)
        onehot = jnp.where(which == batch[0:1, :], 1.0, 0.0)
        loss = scale[0] * lax.dot_general(
            jnp.broadcast_to(persq, (8, n)),
            onehot,
            ROWS,
            precision=lax.Precision.HIGHEST,
            preferred_element_type=jnp.float32,
        )
        for side in (0, 128):
            sent_a[2048:, side : side + 128] = loss
            loss_ref[:, side : side + 128] = loss

    def backward(n):
        piece = step - 8
        for part in range(2):
            rows = slice(part * 256, (part + 1) * 256)
            dhid = jnp.dot(wout_ref[rows, :], dtend_ref[:, :n], preferred_element_type=jnp.float32)
            slope = slope_ref[pl.ds(pl.multiple_of(piece * 512 + part * 256, 256), 256), :n]
            dpre = (dhid * slope).astype(jnp.bfloat16)
            dpre_ref[part * 4 : (part + 1) * 4, :, :, :n] = dpre.reshape(4, 2, 32, n)
        base = piece * 8
        here = hidden_ref.at[pl.ds(base, 8)]
        put_rows(table_ref, here, base, dtn_ref[:n, :], slice(0, 128), kept, sent)
        put_rows(table_ref, dpre_ref, base, xn_ref[:n, :], slice(128, 256), kept, sent)

    pl.when(step == 0)(lambda: by_width(scalar_ref, cols, start))
    pl.when(step < 8)(lambda: by_width(scalar_ref, cols, forward))
    pl.when(step == 7)(lambda: by_width(scalar_ref, cols, middle))
    pl.when(step >= 8)(lambda: by_width(scalar_ref, cols, backward))


def in_hbm(value):
    return pltpu.with_memory_space_constraint(value, pltpu.HBM)


def whole(*shape):
    return pl.BlockSpec(shape, lambda i, *_: (0,) * len(shape), pipeline_mode=pl.Buffered(1))


def shaped(dtype, *shape):
    return jax.ShapeDtypeStruct(shape, dtype)


def params(megabytes):
    return pltpu.CompilerParams(dimension_semantics=("arbitrary",), vmem_limit_bytes=megabytes * 2**20)


def ranks_kernel(mask_ref, batch_ref, ranks_ref, batches_ref, land_ref):
    mask = mask_ref[...]
    ones = mask.astype(jnp.float32)
    first = lax.broadcasted_iota(jnp.int32, (128, 128), 0) < lax.broadcasted_iota(jnp.int32, (128, 128), 1)
    before = jnp.where(first, 1.0, 0.0).astype(jnp.bfloat16)
    within = jnp.dot(ones.astype(jnp.bfloat16), before, preferred_element_type=jnp.float32)
    batch = batch_ref[...].astype(jnp.float32)
    above = jnp.zeros((1, 1), jnp.float32)
    for row in range(8):
        lanes = slice(row * 128, (row + 1) * 128)
        rank = (within[row : row + 1, :] + above).astype(jnp.int32)
        ranks_ref[:, lanes] = jnp.where(mask[row : row + 1, :] > 0, rank, -1)
        batches_ref[:, lanes] = jnp.broadcast_to(batch[row : row + 1, :], (8, 128)).astype(jnp.bfloat16)
        above += jnp.sum(ones[row : row + 1, :], axis=1, keepdims=True)
    land_ref[0] = jnp.sum(ones).astype(jnp.int32)


def land_ranks(mask, batch):
    cols = mask.size
    return pl.pallas_call(
        ranks_kernel,
        in_specs=[pl.BlockSpec(memory_space=pltpu.VMEM)] * 2,
        out_specs=[pl.BlockSpec(memory_space=pltpu.VMEM)] * 2 + [pl.BlockSpec(memory_space=pltpu.SMEM)],
        out_shape=[shaped(jnp.int32, 1, cols), shaped(jnp.bfloat16, 8, cols), shaped(jnp.int32, 1)],
        compiler_params=pltpu.CompilerParams(vmem_limit_bytes=2**21),
        cost_estimate=pl.CostEstimate(flops=2**20, bytes_accessed=2**16, transcendentals=0),
        name="ranks",
    )(mask, batch)


def network(x, field, target, mask, batch, w_in, w_out, total, places):
    feats, cols = x.shape
    hid = w_out.shape[0]
    ranks, batch, land = land_ranks(mask, batch)
    table = jnp.asarray(ring_rows())
    f32, bf16 = jnp.float32, jnp.bfloat16
    tail = [2048, 2048, 2048, 2056, 2048, 2048]
    new, *halves = pl.pallas_call(
        functools.partial(network_kernel, (BATCHES / (total * feats), total ** (-0.5))),
        grid_spec=pltpu.PrefetchScalarGridSpec(
            num_scalar_prefetch=2,
            grid=(16,),
            in_specs=[
                whole(feats, cols),
                pl.BlockSpec((feats, 512), lambda i, *_: (0, jnp.minimum(i, 7))),
                pl.BlockSpec((512, feats), lambda i, *_: (jnp.minimum(i, 7), 0)),
                pl.BlockSpec((512, feats), lambda i, *_: (jnp.maximum(i - 8, 0), 0)),
                whole(feats, cols),
                whole(1, cols),
                whole(8, cols),
                whole(feats, cols),
            ],
            out_specs=[whole(feats * 8, cols // 8)]
            + [whole(size, 256) for size in tail + [8]],
            scratch_shapes=[
                pltpu.VMEM((hid, cols), f32),
                pltpu.VMEM((64, 2, 32, cols), bf16),
                pltpu.VMEM((feats, cols), f32),
                pltpu.VMEM((cols, cols), bf16),
                pltpu.VMEM((feats, cols), bf16),
                pltpu.VMEM((cols, feats), bf16),
                pltpu.VMEM((feats, cols), bf16),
                pltpu.VMEM((cols, feats), bf16),
                pltpu.VMEM((8, 2, 32, cols), bf16),
            ],
        ),
        out_shape=[shaped(f32, feats * 8, cols // 8)] + [shaped(f32, size, 256) for size in tail + [8]],
        compiler_params=params(58),
        cost_estimate=pl.CostEstimate(
            flops=10 * cols * feats * hid, bytes_accessed=20 * 2**20, transcendentals=cols * hid
        ),
        name="network",
    )(land, table, in_hbm(x), w_in, w_out, w_out, target, ranks, batch, in_hbm(field))
    streams = [[kept, lax.ppermute(sent, CORE, PAIR)] for kept, sent in zip(halves[:3], halves[3:6])]
    losses = halves[6] + streams[0][1][2048:]
    for stage in range(3):
        for turn in range(2):
            streams, losses = ring_round(streams, stage, turn, places, losses)
    grad_out = jnp.concatenate([part[:, :128] for (part,) in streams], axis=1)
    grad_in = jnp.concatenate([part[:, 128:] for (part,) in streams], axis=1)
    return new, grad_in, grad_out, losses[0, :BATCHES]


def on_device(state, target, land_mask, batch_map, diffusion, speed_x, speed_y, w_in, w_out):
    feats, rows_x, rows_y = state.shape
    field, x, strips = transported(state, diffusion, speed_x, speed_y)
    target, land_mask, batch_map, *_ = lax.optimization_barrier((target, land_mask, batch_map, *strips))
    local_cols = rows_x * rows_y
    total = local_cols * lax.axis_size(BX) * lax.axis_size(BY)
    new, grad_in, grad_out, batch_loss = network(
        x,
        field,
        target.reshape(feats, local_cols),
        land_mask,
        batch_map,
        w_in,
        w_out,
        total,
        ring_places(),
    )
    return (new.reshape(feats, rows_x, rows_y), grad_in, grad_out, batch_loss)


def solution(mesh):
    torus = Mesh(mesh.devices.reshape(2, 4, 4, 2, 2), BX + BY)
    return jax.shard_map(
        on_device,
        mesh=torus,
        in_specs=(P(None, BX, BY), P(None, BX, BY), P(BX, BY), P(BX, BY), P(), P(), P(), P(), P()),
        out_specs=(P(None, BX, BY), P(BX + BY, None), P(BX + BY, None), P()),
        check_vma=False,
    )
```

```python
import functools

import jax
import jax.numpy as jnp
import numpy as np
from jax import lax
from jax.experimental import pallas as pl
from jax.experimental.pallas import tpu as pltpu
from jax.sharding import Mesh
from jax.sharding import PartitionSpec as P

SUB = 3
BATCHES = 64
FEW = 640
BX = ("bx_0", "bx_1")
BY = ("by_0", "by_1", "by_2")
CORE = "by_2"
AXES = {"x": ("by_0", CORE), "y": ("bx_0", "by_1", CORE), "z": ("bx_1", CORE)}
ORDERS = ("xyz", "yzx", "zxy")
DIGITS = ((0, 3, 1, 2), (0, 1, 2, 3))
RING = {
    1: [(2 * p + c, 2 * (p ^ 1 if c == 0 else 3 - p) + c) for p in range(4) for c in range(2)],
    2: [(2 * p + c, 2 * (3 - p if c == 0 else p ^ 1) + c) for p in range(4) for c in range(2)],
}
PAIR = [(0, 1), (1, 0)]


def edge_kernel(state_ref, low_ref, high_ref, left_ref, right_ref):
    for row in range(8):
        cells = state_ref[pl.ds(row, 128, stride=8), :]
        if row < SUB:
            low_ref[0, row * 128 : (row + 1) * 128, :] = cells
        if row >= 8 - SUB:
            high_ref[0, (row - 8 + SUB) * 128 : (row - 7 + SUB) * 128, :] = cells
        turned = cells.T
        left_ref[0, row * 8 : (row + 1) * 8, :] = turned[:8, :]
        right_ref[0, row * 8 : (row + 1) * 8, :] = turned[120:, :]


def transport_kernel(
    state_ref, above_ref, below_ref, left_ref, right_ref,
    coef_0, coef_1, coef_2, coef_3, coef_4, field_ref, x_ref, even_ref, odd_ref,
):
    lane = lax.broadcasted_iota(jnp.int32, (128, 128), 1)
    gap = jnp.zeros((112, 128), jnp.float32)
    at_x, at_y = lax.axis_index(BX), lax.axis_index(BY)
    inside = [jnp.where(at_x > 0, 1.0, 0.0), jnp.where(at_x < lax.axis_size(BX) - 1, 1.0, 0.0)]
    beside = jnp.where(
        lane < 64, jnp.where(at_y < lax.axis_size(BY) - 1, 1.0, 0.0), jnp.where(at_y > 0, 1.0, 0.0)
    )
    for row in range(-SUB, 8 + SUB):
        if 0 <= row < 8:
            cells = state_ref[pl.ds(row, 128, stride=8), :]
            left, right = (ref[0, row * 8 : (row + 1) * 8, :] for ref in (left_ref, right_ref))
        else:
            far_ref, at = (above_ref, row + SUB) if row < 0 else (below_ref, row - 8)
            cells = far_ref[0, at * 128 : (at + 1) * 128, :]
            left, right = (
                far_ref[0, side + at * 8 : side + (at + 1) * 8, :]
                for side in (SUB * 128, SUB * 136)
            )
        even_ref[row + SUB, 0] = cells
        even_ref[row + SUB, 1] = jnp.concatenate([right, gap, left], axis=0).T
    here, there = even_ref, odd_ref
    for substep in range(SUB):
        margin = SUB - substep - 1
        for row in range(-margin, 8 + margin):
            at = row + SUB
            main, side = here[at, 0], here[at, 1]
            main_up, side_up = pltpu.roll(main, 127, 1), pltpu.roll(side, 127, 1)
            main_down, side_down = pltpu.roll(main, 1, 1), pltpu.roll(side, 1, 1)
            new = (
                coef_0[...] * main
                + coef_1[...] * here[at + 1, 0]
                + coef_2[...] * here[at - 1, 0]
                + coef_3[...] * jnp.where(lane == 127, side_up, main_up)
                + coef_4[...] * jnp.where(lane == 0, side_down, main_down)
            )
            if margin == 0:
                field_ref[:, row * 128 : (row + 1) * 128] = new
                x_ref[:, row * 128 : (row + 1) * 128] = new.astype(jnp.bfloat16)
                continue
            near = (
                coef_0[...] * side
                + coef_1[...] * here[at + 1, 1]
                + coef_2[...] * here[at - 1, 1]
                + coef_3[...] * jnp.where(lane == 127, main_up, side_up)
                + coef_4[...] * jnp.where(lane == 0, main_down, side_down)
            ) * beside
            if row < 0 or row > 7:
                new = new * inside[0 if row < 0 else 1]
                near = near * inside[0 if row < 0 else 1]
            there[at, 0] = new
            there[at, 1] = near
        here, there = there, here


def shifted(value, axis, step):
    count = lax.axis_size(axis)
    pairs = [(i, i + step) for i in range(count) if 0 <= i + step < count]
    return lax.ppermute(value, axis, pairs)


def transported(state, diffusion, speed_x, speed_y):
    feats = state.shape[0]
    f32 = jnp.float32
    flat = in_hbm(state.reshape(feats * 8, 128))
    chunk = lambda rows: pl.BlockSpec((1, rows, 128), lambda i: (i, 0, 0))
    low, high, left, right = pl.pallas_call(
        edge_kernel,
        grid=(feats // 128,),
        in_specs=[pl.BlockSpec((1024, 128), lambda i: (i, 0))],
        out_specs=[chunk(SUB * 144), chunk(SUB * 144), chunk(64), chunk(64)],
        out_shape=[shaped(f32, feats // 128, rows, 128) for rows in (SUB * 144, SUB * 144, 64, 64)],
        compiler_params=params(16),
        cost_estimate=pl.CostEstimate(flops=2**20, bytes_accessed=3 * 2**20, transcendentals=0),
        name="edges",
    )(flat)
    from_left = shifted(right, BY, 1)
    from_right = shifted(left, BY, -1)
    low, high = (
        lax.dynamic_update_slice(
            edge, jnp.concatenate([from_left[:, rows], from_right[:, rows]], axis=1), (0, SUB * 128, 0)
        )
        for edge, rows in ((low, slice(0, SUB * 8)), (high, slice((8 - SUB) * 8, 64)))
    )
    above = shifted(high, BX, 1)
    below = shifted(low, BX, -1)
    coefs = [
        jnp.broadcast_to(value[:, None], (feats, 128))
        for value in (
            1.0 - 4.0 * diffusion,
            diffusion - 0.5 * speed_x,
            diffusion + 0.5 * speed_x,
            diffusion - 0.5 * speed_y,
            diffusion + 0.5 * speed_y,
        )
    ]
    field, x = pl.pallas_call(
        transport_kernel,
        grid=(feats // 128,),
        in_specs=[
            pl.BlockSpec((1024, 128), lambda i: (i, 0)),
            chunk(SUB * 144),
            chunk(SUB * 144),
            chunk(64),
            chunk(64),
        ]
        + [pl.BlockSpec((128, 128), lambda i: (i, 0))] * 5,
        out_specs=[pl.BlockSpec((128, 1024), lambda i: (i, 0))] * 2,
        scratch_shapes=[pltpu.VMEM((14, 2, 128, 128), f32)] * 2,
        out_shape=[pltpu.HBM((feats, 1024), f32), pltpu.HBM((feats, 1024), jnp.bfloat16)],
        compiler_params=params(16),
        cost_estimate=pl.CostEstimate(flops=2**24, bytes_accessed=6 * 2**20, transcendentals=0),
        name="transport",
    )(flat, above, below, from_left, from_right, *coefs)
    return field, x, (from_left, from_right)


def position(axis):
    if axis == "y":
        return lax.axis_index("bx_0") * 2 + lax.axis_index("by_1")
    return lax.axis_index("by_0" if axis == "x" else "bx_1")


def ring_places():
    core = lax.axis_index(CORE)
    places = {}
    for axis in "xyz":
        at = position(axis)
        folded = jnp.where(at == 0, 0, jnp.where(at == 3, 1, at + 1))
        places[axis] = jnp.where(core == 0, folded, at)
    return places


def half_of(rows, size, bit):
    return lax.dynamic_slice_in_dim(rows, bit * size, size, 0)


def ring_turn(terms, axis, turn, places, riding=None):
    bit = places[axis] % 2 if turn else places[axis] // 2
    size = terms[0].shape[0] // 2
    leaving = sum(half_of(term, size, 1 - bit) for term in terms)
    if riding is not None:
        leaving = jnp.concatenate([leaving, riding], axis=0)
    coming = lax.ppermute(leaving, AXES[axis], RING[turn + 1])
    staying = sum(half_of(term, size, bit) for term in terms)
    return [staying + coming[:size]], (None if riding is None else riding + coming[size:])


def ring_round(streams, stage, turn, places, riding=None):
    moved = []
    for stream, order in enumerate(ORDERS):
        terms, carried = ring_turn(
            streams[stream], order[stage], turn, places, riding if stream == 0 else None
        )
        riding = carried if stream == 0 else riding
        moved.append(terms)
    return moved, riding


def ring_rows():
    table = np.zeros((2, len(ORDERS), 64), np.int32)
    for core in range(2):
        for block in range(64):
            y_hi, z, x, y_lo = block // 32, block // 8 % 4, block // 2 % 4, block % 2
            at = {"x": x, "y": 2 * y_hi + y_lo, "z": z}
            for stream, order in enumerate(ORDERS):
                spot = 0
                for axis in order:
                    spot = spot * 4 + DIGITS[core].index(at[axis])
                table[core, stream, block] = spot * 32
    return table.reshape(-1)


def by_width(scalar_ref, most, body):
    land = scalar_ref[0]
    pl.when(land <= FEW)(functools.partial(body, FEW))
    pl.when(land > FEW)(functools.partial(body, most))


ROWS = (((1,), (1,)), ((), ()))


def network_kernel(
    scale, scalar_ref, table_ref, x_hbm, win_hbm, wout_hbm, target_hbm, field_hbm, rank_ref, batch_ref,
    new_hbm, kept_hbm_a, kept_hbm_b, kept_hbm_c, sent_hbm_a, sent_hbm_b, sent_hbm_c, loss_ref,
    x_ref, win_ref, wout_ref, target_ref, field_ref, new_ref, kept_a, kept_b, kept_c, sent_a, sent_b, sent_c,
    slope_ref, hidden_ref, tend_ref, pick_ref, xc_ref, xn_ref, dtend_ref, dtn_ref,
    win_sem, wout_sem, in_sem, out_sem,
):
    feats, cols = x_ref.shape
    core = lax.axis_index(CORE)
    incoming = [
        pltpu.make_async_copy(source, ref, in_sem.at[k])
        for k, (source, ref) in enumerate(((x_hbm, x_ref), (target_hbm, target_ref), (field_hbm, field_ref)))
    ]
    outgoing = [
        pltpu.make_async_copy(ref, dest, out_sem.at[k])
        for k, (ref, dest) in enumerate(
            (
                (new_ref, new_hbm),
                (sent_a, sent_hbm_a),
                (sent_b, sent_hbm_b),
                (sent_c, sent_hbm_c),
                (kept_a, kept_hbm_a),
                (kept_b, kept_hbm_b),
                (kept_c, kept_hbm_c),
            )
        )
    ]

    def win_copy(piece):
        return pltpu.make_async_copy(
            win_hbm.at[:, pl.ds(pl.multiple_of(piece * 512, 512), 512)], win_ref.at[piece], win_sem.at[piece]
        )

    def wout_copy(piece):
        at = pl.ds(piece * 8, 8)
        return pltpu.make_async_copy(wout_hbm.at[at], wout_ref.at[at], wout_sem.at[piece])

    incoming[0].start()
    for piece in range(8):
        win_copy(piece).start()
        wout_copy(piece).start()
    incoming[1].start()
    incoming[2].start()

    def run(n):
        for at in range(0, n, 128):
            slot = lax.broadcasted_iota(jnp.int32, (128, cols), 0) + at
            pick_ref[at : at + 128, :] = jnp.where(slot == rank_ref[...], 1.0, 0.0).astype(jnp.bfloat16)
        incoming[0].wait()
        packed = lax.dot_general(x_ref[...], pick_ref[:n, :], ROWS, preferred_element_type=jnp.float32)
        packed = packed.astype(jnp.bfloat16)
        xc_ref[:, :n] = packed
        xn_ref[:n, :] = packed.T
        tend_ref[:, :n] = jnp.zeros((feats, n), jnp.float32)

        def activate(piece):
            for part in range(2):
                rows = slice(part * 256, (part + 1) * 256)
                pre = jnp.dot(win_ref[piece, :, rows].T, xc_ref[:, :n], preferred_element_type=jnp.float32)
                sig = 0.5 * jnp.tanh(0.5 * pre) + 0.5
                act = pre * sig
                at = pl.ds(piece * 8 + part * 4, 4)
                slope_ref[at, :, :, :n] = (sig + act * (1.0 - sig)).reshape(4, 2, 32, n)
                hidden_ref[at, :, :, :n] = act.astype(jnp.bfloat16).reshape(4, 2, 32, n)

        def project(piece):
            at = pl.ds(piece * 8, 8)
            tend_ref[:, :n] += jnp.dot(
                wout_ref[at].reshape(512, feats).T,
                hidden_ref[at, :, :, :n].reshape(512, n),
                preferred_element_type=jnp.float32,
            )

        win_copy(0).wait()
        activate(0)

        @pl.loop(1, 8)
        def _(piece):
            win_copy(piece).wait()
            wout_copy(piece - 1).wait()
            project(piece - 1)
            activate(piece)

        wout_copy(7).wait()
        project(7)
        pick = pick_ref[:n, :]
        tend = tend_ref[:, :n]
        incoming[1].wait()
        wanted = lax.dot_general(target_ref[...], pick, ROWS, preferred_element_type=jnp.float32)
        err = tend - wanted
        dtend = (err * scale[1]).astype(jnp.bfloat16)
        dtend_ref[:, :n] = dtend
        dtn_ref[:n, :] = dtend.T
        coarse = tend.astype(jnp.bfloat16)
        fine = (tend - coarse.astype(jnp.float32)).astype(jnp.bfloat16)
        spread = jnp.dot(coarse, pick, preferred_element_type=jnp.float32)
        spread += jnp.dot(fine, pick, preferred_element_type=jnp.float32)
        incoming[2].wait()
        new = field_ref[...] + 0.5 * spread
        for row in range(8):
            new_ref[pl.ds(row, feats, stride=8), :] = new[:, row * 128 : (row + 1) * 128]
        outgoing[0].start()
        persq = 0.5 * jnp.sum(err * err, axis=0, keepdims=True)
        batch = lax.dot_general(batch_ref[...], pick, ROWS, preferred_element_type=jnp.float32)
        which = lax.broadcasted_iota(jnp.int32, (128, n), 0).astype(jnp.float32)
        onehot = jnp.where(which == batch[0:1, :], 1.0, 0.0)
        loss = scale[0] * lax.dot_general(
            jnp.broadcast_to(persq, (8, n)),
            onehot,
            ROWS,
            precision=lax.Precision.HIGHEST,
            preferred_element_type=jnp.float32,
        )
        for side in (0, 128):
            sent_a[2048:, side : side + 128] = loss
            loss_ref[:, side : side + 128] = loss

        for digit, out_refs, copies in (
            (1 - core, (sent_a, sent_b, sent_c), outgoing[1:4]),
            (core, (kept_a, kept_b, kept_c), outgoing[4:]),
        ):

            @pl.loop(0, 4)
            def _(piece, digit=digit, out_refs=out_refs):
                at = pl.ds(piece * 16, 16)
                dhid = jnp.dot(
                    wout_ref[at, digit].reshape(512, feats), dtend_ref[:, :n], preferred_element_type=jnp.float32
                )
                dpre = (dhid * slope_ref[at, digit, :, :n].reshape(512, n)).astype(jnp.bfloat16)
                sums = (
                    jnp.dot(
                        hidden_ref[at, digit, :, :n].reshape(512, n), dtn_ref[:n, :], preferred_element_type=jnp.float32
                    ),
                    jnp.dot(dpre, xn_ref[:n, :], preferred_element_type=jnp.float32),
                )
                for block in range(16):
                    for stream in range(3):
                        row = table_ref[digit * 192 + stream * 64 + piece * 16 + block]
                        for which in range(2):
                            out_refs[stream][
                                pl.ds(pl.multiple_of(row, 32), 32), which * 128 : (which + 1) * 128
                            ] = sums[which][block * 32 : (block + 1) * 32, stream * 128 : (stream + 1) * 128]

            for copy in copies:
                copy.start()

    by_width(scalar_ref, cols, run)
    for copy in outgoing:
        copy.wait()


def in_hbm(value):
    return pltpu.with_memory_space_constraint(value, pltpu.HBM)


def whole(*shape):
    return pl.BlockSpec(shape, lambda i, *_: (0,) * len(shape), pipeline_mode=pl.Buffered(1))


def shaped(dtype, *shape):
    return jax.ShapeDtypeStruct(shape, dtype)


def params(megabytes):
    return pltpu.CompilerParams(dimension_semantics=("arbitrary",), vmem_limit_bytes=megabytes * 2**20)


def ranks_kernel(mask_ref, batch_ref, ranks_ref, batches_ref, land_ref):
    mask = mask_ref[...]
    ones = mask.astype(jnp.float32)
    first = lax.broadcasted_iota(jnp.int32, (128, 128), 0) < lax.broadcasted_iota(jnp.int32, (128, 128), 1)
    before = jnp.where(first, 1.0, 0.0).astype(jnp.bfloat16)
    within = jnp.dot(ones.astype(jnp.bfloat16), before, preferred_element_type=jnp.float32)
    batch = batch_ref[...].astype(jnp.float32)
    above = jnp.zeros((1, 1), jnp.float32)
    for row in range(8):
        lanes = slice(row * 128, (row + 1) * 128)
        rank = (within[row : row + 1, :] + above).astype(jnp.int32)
        ranks_ref[:, lanes] = jnp.where(mask[row : row + 1, :] > 0, rank, -1)
        batches_ref[:, lanes] = jnp.broadcast_to(batch[row : row + 1, :], (8, 128)).astype(jnp.bfloat16)
        above += jnp.sum(ones[row : row + 1, :], axis=1, keepdims=True)
    land_ref[0] = jnp.sum(ones).astype(jnp.int32)


def land_ranks(mask, batch):
    cols = mask.size
    return pl.pallas_call(
        ranks_kernel,
        in_specs=[pl.BlockSpec(memory_space=pltpu.VMEM)] * 2,
        out_specs=[pl.BlockSpec(memory_space=pltpu.VMEM)] * 2 + [pl.BlockSpec(memory_space=pltpu.SMEM)],
        out_shape=[shaped(jnp.int32, 1, cols), shaped(jnp.bfloat16, 8, cols), shaped(jnp.int32, 1)],
        compiler_params=pltpu.CompilerParams(vmem_limit_bytes=2**21),
        cost_estimate=pl.CostEstimate(flops=2**20, bytes_accessed=2**16, transcendentals=0),
        name="ranks",
    )(mask, batch)


def network(x, field, target, mask, batch, w_in, w_out, total, places):
    feats, cols = x.shape
    hid = w_out.shape[0]
    ranks, batch, land = land_ranks(mask, batch)
    table = jnp.asarray(ring_rows())
    f32, bf16 = jnp.float32, jnp.bfloat16
    tail = [2048, 2048, 2048, 2056, 2048, 2048]
    hbm = pl.BlockSpec(memory_space=pl.ANY)
    vmem = pl.BlockSpec(memory_space=pltpu.VMEM)
    smem = pl.BlockSpec(memory_space=pltpu.SMEM)
    new, *halves = pl.pallas_call(
        functools.partial(network_kernel, (BATCHES / (total * feats), total ** (-0.5))),
        in_specs=[smem, smem, hbm, hbm, hbm, hbm, hbm, vmem, vmem],
        out_specs=[hbm] * 7 + [vmem],
        scratch_shapes=[
            pltpu.VMEM((feats, cols), bf16),
            pltpu.VMEM((8, feats, 512), bf16),
            pltpu.VMEM((64, 2, 32, feats), bf16),
            pltpu.VMEM((feats, cols), bf16),
            pltpu.VMEM((feats, cols), f32),
            pltpu.VMEM((feats * 8, cols // 8), f32),
        ]
        + [pltpu.VMEM((size, 256), f32) for size in tail]
        + [
            pltpu.VMEM((64, 2, 32, cols), f32),
            pltpu.VMEM((64, 2, 32, cols), bf16),
            pltpu.VMEM((feats, cols), f32),
            pltpu.VMEM((cols, cols), bf16),
            pltpu.VMEM((feats, cols), bf16),
            pltpu.VMEM((cols, feats), bf16),
            pltpu.VMEM((feats, cols), bf16),
            pltpu.VMEM((cols, feats), bf16),
            pltpu.SemaphoreType.DMA((8,)),
            pltpu.SemaphoreType.DMA((8,)),
            pltpu.SemaphoreType.DMA((3,)),
            pltpu.SemaphoreType.DMA((7,)),
        ],
        out_shape=[shaped(f32, feats * 8, cols // 8)] + [shaped(f32, size, 256) for size in tail + [8]],
        compiler_params=pltpu.CompilerParams(vmem_limit_bytes=60 * 2**20),
        cost_estimate=pl.CostEstimate(
            flops=10 * cols * feats * hid, bytes_accessed=20 * 2**20, transcendentals=cols * hid
        ),
        name="network",
    )(land, table, x, w_in, w_out.reshape(64, 2, 32, feats), target, field, ranks, batch)
    streams = [[kept, lax.ppermute(sent, CORE, PAIR)] for kept, sent in zip(halves[:3], halves[3:6])]
    losses = halves[6] + streams[0][1][2048:]
    for stage in range(3):
        for turn in range(2):
            streams, losses = ring_round(streams, stage, turn, places, losses)
    grad_out = jnp.concatenate([part[:, :128] for (part,) in streams], axis=1)
    grad_in = jnp.concatenate([part[:, 128:] for (part,) in streams], axis=1)
    return new, grad_in, grad_out, losses[0, :BATCHES]


def on_device(state, target, land_mask, batch_map, diffusion, speed_x, speed_y, w_in, w_out):
    feats, rows_x, rows_y = state.shape
    field, x, strips = transported(state, diffusion, speed_x, speed_y)
    target, land_mask, batch_map, *_ = lax.optimization_barrier((target, land_mask, batch_map, *strips))
    local_cols = rows_x * rows_y
    total = local_cols * lax.axis_size(BX) * lax.axis_size(BY)
    new, grad_in, grad_out, batch_loss = network(
        x,
        field,
        target.reshape(feats, local_cols),
        land_mask,
        batch_map,
        w_in,
        w_out,
        total,
        ring_places(),
    )
    return (new.reshape(feats, rows_x, rows_y), grad_in, grad_out, batch_loss)


def solution(mesh):
    torus = Mesh(mesh.devices.reshape(2, 4, 4, 2, 2), BX + BY)
    return jax.shard_map(
        on_device,
        mesh=torus,
        in_specs=(P(None, BX, BY), P(None, BX, BY), P(BX, BY), P(BX, BY), P(), P(), P(), P(), P()),
        out_specs=(P(None, BX, BY), P(BX + BY, None), P(BX + BY, None), P()),
        check_vma=False,
    )
```

```python
import functools

import jax
import jax.numpy as jnp
import numpy as np
from jax import lax
from jax.experimental import pallas as pl
from jax.experimental.pallas import tpu as pltpu
from jax.sharding import Mesh
from jax.sharding import PartitionSpec as P

SUB = 3
BATCHES = 64
FEW = 640
FEW_ROWS = 32
BX = ("bx_0", "bx_1")
BY = ("by_0", "by_1", "by_2")
CORE = "by_2"
AXES = {"x": ("by_0", CORE), "y": ("bx_0", "by_1", CORE), "z": ("bx_1", CORE)}
ORDERS = ("xyz", "yzx", "zxy")
DIGITS = ((0, 3, 1, 2), (0, 1, 2, 3))
RING = {
    1: [(2 * p + c, 2 * (p ^ 1 if c == 0 else 3 - p) + c) for p in range(4) for c in range(2)],
    2: [(2 * p + c, 2 * (3 - p if c == 0 else p ^ 1) + c) for p in range(4) for c in range(2)],
}
PAIR = [(0, 1), (1, 0)]


def edge_kernel(state_ref, low_ref, high_ref, left_ref, right_ref):
    for row in range(8):
        cells = state_ref[pl.ds(row, 128, stride=8), :]
        if row < SUB:
            low_ref[0, row * 128 : (row + 1) * 128, :] = cells
        if row >= 8 - SUB:
            high_ref[0, (row - 8 + SUB) * 128 : (row - 7 + SUB) * 128, :] = cells
        turned = cells.T
        left_ref[0, row * 8 : (row + 1) * 8, :] = turned[:8, :]
        right_ref[0, row * 8 : (row + 1) * 8, :] = turned[120:, :]


def transport_kernel(
    state_ref, above_ref, below_ref, left_ref, right_ref,
    coef_0, coef_1, coef_2, coef_3, coef_4, field_ref, x_ref, even_ref, odd_ref,
):
    lane = lax.broadcasted_iota(jnp.int32, (128, 128), 1)
    gap = jnp.zeros((112, 128), jnp.float32)
    at_x, at_y = lax.axis_index(BX), lax.axis_index(BY)
    inside = [jnp.where(at_x > 0, 1.0, 0.0), jnp.where(at_x < lax.axis_size(BX) - 1, 1.0, 0.0)]
    beside = jnp.where(
        lane < 64, jnp.where(at_y < lax.axis_size(BY) - 1, 1.0, 0.0), jnp.where(at_y > 0, 1.0, 0.0)
    )
    for row in range(-SUB, 8 + SUB):
        if 0 <= row < 8:
            cells = state_ref[pl.ds(row, 128, stride=8), :]
            left, right = (ref[0, row * 8 : (row + 1) * 8, :] for ref in (left_ref, right_ref))
        else:
            far_ref, at = (above_ref, row + SUB) if row < 0 else (below_ref, row - 8)
            cells = far_ref[0, at * 128 : (at + 1) * 128, :]
            left, right = (
                far_ref[0, side + at * 8 : side + (at + 1) * 8, :]
                for side in (SUB * 128, SUB * 136)
            )
        even_ref[row + SUB, 0] = cells
        even_ref[row + SUB, 1] = jnp.concatenate([right, gap, left], axis=0).T
    lane = lane[:FEW_ROWS]
    beside = beside[:FEW_ROWS]

    @pl.loop(0, 128 // FEW_ROWS)
    def _(piece):
        feats = pl.ds(pl.multiple_of(piece * FEW_ROWS, FEW_ROWS), FEW_ROWS)
        centre, east, west, north, south = (ref[feats, :] for ref in (coef_0, coef_1, coef_2, coef_3, coef_4))
        here, there = even_ref, odd_ref
        for substep in range(SUB):
            margin = SUB - substep - 1
            for row in range(-margin, 8 + margin):
                at = row + SUB
                main, side = here[at, 0, feats, :], here[at, 1, feats, :]
                main_up, side_up = pltpu.roll(main, 127, 1), pltpu.roll(side, 127, 1)
                main_down, side_down = pltpu.roll(main, 1, 1), pltpu.roll(side, 1, 1)
                new = (
                    centre * main
                    + east * here[at + 1, 0, feats, :]
                    + west * here[at - 1, 0, feats, :]
                    + north * jnp.where(lane == 127, side_up, main_up)
                    + south * jnp.where(lane == 0, side_down, main_down)
                )
                if margin == 0:
                    field_ref[feats, row * 128 : (row + 1) * 128] = new
                    x_ref[feats, row * 128 : (row + 1) * 128] = new.astype(jnp.bfloat16)
                    continue
                near = (
                    centre * side
                    + east * here[at + 1, 1, feats, :]
                    + west * here[at - 1, 1, feats, :]
                    + north * jnp.where(lane == 127, main_up, side_up)
                    + south * jnp.where(lane == 0, main_down, side_down)
                ) * beside
                if row < 0 or row > 7:
                    new = new * inside[0 if row < 0 else 1]
                    near = near * inside[0 if row < 0 else 1]
                there[at, 0, feats, :] = new
                there[at, 1, feats, :] = near
            here, there = there, here


def shifted(value, axis, step):
    count = lax.axis_size(axis)
    pairs = [(i, i + step) for i in range(count) if 0 <= i + step < count]
    return lax.ppermute(value, axis, pairs)


def transported(state, diffusion, speed_x, speed_y):
    feats = state.shape[0]
    f32 = jnp.float32
    flat = in_hbm(state.reshape(feats * 8, 128))
    chunk = lambda rows: pl.BlockSpec((1, rows, 128), lambda i: (i, 0, 0))
    low, high, left, right = pl.pallas_call(
        edge_kernel,
        grid=(feats // 128,),
        in_specs=[pl.BlockSpec((1024, 128), lambda i: (i, 0))],
        out_specs=[chunk(SUB * 144), chunk(SUB * 144), chunk(64), chunk(64)],
        out_shape=[shaped(f32, feats // 128, rows, 128) for rows in (SUB * 144, SUB * 144, 64, 64)],
        compiler_params=params(16),
        cost_estimate=pl.CostEstimate(flops=2**20, bytes_accessed=3 * 2**20, transcendentals=0),
        name="edges",
    )(flat)
    from_left = shifted(right, BY, 1)
    from_right = shifted(left, BY, -1)
    low, high = (
        lax.dynamic_update_slice(
            edge, jnp.concatenate([from_left[:, rows], from_right[:, rows]], axis=1), (0, SUB * 128, 0)
        )
        for edge, rows in ((low, slice(0, SUB * 8)), (high, slice((8 - SUB) * 8, 64)))
    )
    above = shifted(high, BX, 1)
    below = shifted(low, BX, -1)
    coefs = [
        jnp.broadcast_to(value[:, None], (feats, 128))
        for value in (
            1.0 - 4.0 * diffusion,
            diffusion - 0.5 * speed_x,
            diffusion + 0.5 * speed_x,
            diffusion - 0.5 * speed_y,
            diffusion + 0.5 * speed_y,
        )
    ]
    field, x = pl.pallas_call(
        transport_kernel,
        grid=(feats // 128,),
        in_specs=[
            pl.BlockSpec((1024, 128), lambda i: (i, 0)),
            chunk(SUB * 144),
            chunk(SUB * 144),
            chunk(64),
            chunk(64),
        ]
        + [pl.BlockSpec((128, 128), lambda i: (i, 0))] * 5,
        out_specs=[pl.BlockSpec((128, 1024), lambda i: (i, 0))] * 2,
        scratch_shapes=[pltpu.VMEM((14, 2, 128, 128), f32)] * 2,
        out_shape=[pltpu.HBM((feats, 1024), f32), pltpu.HBM((feats, 1024), jnp.bfloat16)],
        compiler_params=params(16),
        cost_estimate=pl.CostEstimate(flops=2**24, bytes_accessed=6 * 2**20, transcendentals=0),
        name="transport",
    )(flat, above, below, from_left, from_right, *coefs)
    return field, x, (from_left, from_right)


def position(axis):
    if axis == "y":
        return lax.axis_index("bx_0") * 2 + lax.axis_index("by_1")
    return lax.axis_index("by_0" if axis == "x" else "bx_1")


def ring_places():
    core = lax.axis_index(CORE)
    places = {}
    for axis in "xyz":
        at = position(axis)
        folded = jnp.where(at == 0, 0, jnp.where(at == 3, 1, at + 1))
        places[axis] = jnp.where(core == 0, folded, at)
    return places


def half_of(rows, size, bit):
    return lax.dynamic_slice_in_dim(rows, bit * size, size, 0)


def ring_turn(terms, axis, turn, places, riding=None):
    bit = places[axis] % 2 if turn else places[axis] // 2
    size = terms[0].shape[0] // 2
    leaving = sum(half_of(term, size, 1 - bit) for term in terms)
    if riding is not None:
        leaving = jnp.concatenate([leaving, riding], axis=0)
    coming = lax.ppermute(leaving, AXES[axis], RING[turn + 1])
    staying = sum(half_of(term, size, bit) for term in terms)
    return [staying + coming[:size]], (None if riding is None else riding + coming[size:])


def ring_round(streams, stage, turn, places, riding=None):
    moved = []
    for stream, order in enumerate(ORDERS):
        terms, carried = ring_turn(
            streams[stream], order[stage], turn, places, riding if stream == 0 else None
        )
        riding = carried if stream == 0 else riding
        moved.append(terms)
    return moved, riding


def ring_rows():
    table = np.zeros((2, len(ORDERS), 64), np.int32)
    for core in range(2):
        for block in range(64):
            y_hi, z, x, y_lo = block // 32, block // 8 % 4, block // 2 % 4, block % 2
            at = {"x": x, "y": 2 * y_hi + y_lo, "z": z}
            for stream, order in enumerate(ORDERS):
                spot = 0
                for axis in order:
                    spot = spot * 4 + DIGITS[core].index(at[axis])
                table[core, stream, block] = spot * 32
    return table.reshape(-1)


def by_width(scalar_ref, most, body):
    land = scalar_ref[0]
    pl.when(land <= FEW)(functools.partial(body, FEW))
    pl.when(land > FEW)(functools.partial(body, most))


ROWS = (((1,), (1,)), ((), ()))


def network_kernel(
    scale, scalar_ref, table_ref, x_hbm, win_hbm, wout_hbm, target_hbm, field_hbm, rank_ref, batch_ref,
    new_hbm, kept_hbm_a, kept_hbm_b, kept_hbm_c, sent_hbm_a, sent_hbm_b, sent_hbm_c, loss_ref,
    x_ref, win_ref, wout_ref, target_ref, field_ref, new_ref, kept_a, kept_b, kept_c, sent_a, sent_b, sent_c,
    slope_ref, hidden_ref, tend_ref, pick_ref, xc_ref, xn_ref, dtend_ref, dtn_ref, persq_ref,
    win_sem, wout_sem, in_sem, out_sem,
):
    feats, cols = x_ref.shape
    core = lax.axis_index(CORE)
    incoming = [
        pltpu.make_async_copy(source, ref, in_sem.at[k])
        for k, (source, ref) in enumerate(((x_hbm, x_ref), (target_hbm, target_ref), (field_hbm, field_ref)))
    ]
    outgoing = [
        pltpu.make_async_copy(ref, dest, out_sem.at[k])
        for k, (ref, dest) in enumerate(
            (
                (new_ref, new_hbm),
                (sent_a, sent_hbm_a),
                (sent_b, sent_hbm_b),
                (sent_c, sent_hbm_c),
                (kept_a, kept_hbm_a),
                (kept_b, kept_hbm_b),
                (kept_c, kept_hbm_c),
            )
        )
    ]

    def win_copy(piece):
        return pltpu.make_async_copy(
            win_hbm.at[:, pl.ds(pl.multiple_of(piece * 512, 512), 512)], win_ref.at[piece], win_sem.at[piece]
        )

    def wout_copy(piece):
        at = pl.ds(piece * 8, 8)
        return pltpu.make_async_copy(wout_hbm.at[at], wout_ref.at[at], wout_sem.at[piece])

    incoming[0].start()
    for piece in range(8):
        win_copy(piece).start()
        wout_copy(piece).start()
    incoming[1].start()
    incoming[2].start()

    def run(n):
        @pl.loop(0, n // 128)
        def _(block):
            slot = lax.broadcasted_iota(jnp.int32, (128, cols), 0) + block * 128
            pick_ref[pl.ds(pl.multiple_of(block * 128, 128), 128), :] = jnp.where(
                slot == rank_ref[...], 1.0, 0.0
            ).astype(jnp.bfloat16)

        incoming[0].wait()

        @pl.loop(0, feats // 128)
        def _(block):
            some = pl.ds(pl.multiple_of(block * 128, 128), 128)
            packed = lax.dot_general(x_ref[some, :], pick_ref[:n, :], ROWS, preferred_element_type=jnp.float32)
            packed = packed.astype(jnp.bfloat16)
            xc_ref[some, :n] = packed
            xn_ref[:n, some] = packed.T
            tend_ref[some, :n] = jnp.zeros((128, n), jnp.float32)

        def activate(piece):
            for part in range(2):
                rows = slice(part * 256, (part + 1) * 256)
                pre = jnp.dot(win_ref[piece, :, rows].T, xc_ref[:, :n], preferred_element_type=jnp.float32)
                sig = 0.5 * jnp.tanh(0.5 * pre) + 0.5
                act = pre * sig
                at = pl.ds(piece * 8 + part * 4, 4)
                slope_ref[at, :, :, :n] = (sig + act * (1.0 - sig)).reshape(4, 2, 32, n)
                hidden_ref[at, :, :, :n] = act.astype(jnp.bfloat16).reshape(4, 2, 32, n)

        def project(piece):
            at = pl.ds(piece * 8, 8)
            tend_ref[:, :n] += jnp.dot(
                wout_ref[at].reshape(512, feats).T,
                hidden_ref[at, :, :, :n].reshape(512, n),
                preferred_element_type=jnp.float32,
            )

        win_copy(0).wait()
        activate(0)

        @pl.loop(1, 8)
        def _(piece):
            win_copy(piece).wait()
            wout_copy(piece - 1).wait()
            project(piece - 1)
            activate(piece)

        wout_copy(7).wait()
        project(7)
        pick = pick_ref[:n, :]
        persq_ref[:, :n] = jnp.zeros((1, n), jnp.float32)
        incoming[1].wait()
        incoming[2].wait()

        @pl.loop(0, feats // 128)
        def _(block):
            some = pl.ds(pl.multiple_of(block * 128, 128), 128)
            tend = tend_ref[some, :n]
            wanted = lax.dot_general(target_ref[some, :], pick_ref[:n, :], ROWS, preferred_element_type=jnp.float32)
            err = tend - wanted
            persq_ref[:, :n] += 0.5 * jnp.sum(err * err, axis=0, keepdims=True)
            dtend = (err * scale[1]).astype(jnp.bfloat16)
            dtend_ref[some, :n] = dtend
            dtn_ref[:n, some] = dtend.T
            coarse = tend.astype(jnp.bfloat16)
            fine = (tend - coarse.astype(jnp.float32)).astype(jnp.bfloat16)
            spread = jnp.dot(coarse, pick_ref[:n, :], preferred_element_type=jnp.float32)
            spread += jnp.dot(fine, pick_ref[:n, :], preferred_element_type=jnp.float32)
            new = field_ref[some, :] + 0.5 * spread
            for row in range(8):
                new_ref[pl.ds(block * 1024 + row, 128, stride=8), :] = new[:, row * 128 : (row + 1) * 128]

        outgoing[0].start()
        persq = persq_ref[:, :n]
        batch = lax.dot_general(batch_ref[...], pick, ROWS, preferred_element_type=jnp.float32)
        which = lax.broadcasted_iota(jnp.int32, (128, n), 0).astype(jnp.float32)
        onehot = jnp.where(which == batch[0:1, :], 1.0, 0.0)
        loss = scale[0] * lax.dot_general(
            jnp.broadcast_to(persq, (8, n)),
            onehot,
            ROWS,
            precision=lax.Precision.HIGHEST,
            preferred_element_type=jnp.float32,
        )
        for side in (0, 128):
            sent_a[2048:, side : side + 128] = loss
            loss_ref[:, side : side + 128] = loss

        for digit, out_refs, copies in (
            (1 - core, (sent_a, sent_b, sent_c), outgoing[1:4]),
            (core, (kept_a, kept_b, kept_c), outgoing[4:]),
        ):

            @pl.loop(0, 4)
            def _(piece, digit=digit, out_refs=out_refs):
                at = pl.ds(piece * 16, 16)
                dhid = jnp.dot(
                    wout_ref[at, digit].reshape(512, feats), dtend_ref[:, :n], preferred_element_type=jnp.float32
                )
                dpre = (dhid * slope_ref[at, digit, :, :n].reshape(512, n)).astype(jnp.bfloat16)
                sums = (
                    jnp.dot(
                        hidden_ref[at, digit, :, :n].reshape(512, n), dtn_ref[:n, :], preferred_element_type=jnp.float32
                    ),
                    jnp.dot(dpre, xn_ref[:n, :], preferred_element_type=jnp.float32),
                )
                for block in range(16):
                    for stream in range(3):
                        row = table_ref[digit * 192 + stream * 64 + piece * 16 + block]
                        for which in range(2):
                            out_refs[stream][
                                pl.ds(pl.multiple_of(row, 32), 32), which * 128 : (which + 1) * 128
                            ] = sums[which][block * 32 : (block + 1) * 32, stream * 128 : (stream + 1) * 128]

            for copy in copies:
                copy.start()

    by_width(scalar_ref, cols, run)
    for copy in outgoing:
        copy.wait()


def in_hbm(value):
    return pltpu.with_memory_space_constraint(value, pltpu.HBM)


def whole(*shape):
    return pl.BlockSpec(shape, lambda i, *_: (0,) * len(shape), pipeline_mode=pl.Buffered(1))


def shaped(dtype, *shape):
    return jax.ShapeDtypeStruct(shape, dtype)


def params(megabytes):
    return pltpu.CompilerParams(dimension_semantics=("arbitrary",), vmem_limit_bytes=megabytes * 2**20)


def ranks_kernel(mask_ref, batch_ref, ranks_ref, batches_ref, land_ref):
    mask = mask_ref[...]
    ones = mask.astype(jnp.float32)
    first = lax.broadcasted_iota(jnp.int32, (128, 128), 0) < lax.broadcasted_iota(jnp.int32, (128, 128), 1)
    before = jnp.where(first, 1.0, 0.0).astype(jnp.bfloat16)
    within = jnp.dot(ones.astype(jnp.bfloat16), before, preferred_element_type=jnp.float32)
    batch = batch_ref[...].astype(jnp.float32)
    above = jnp.zeros((1, 1), jnp.float32)
    for row in range(8):
        lanes = slice(row * 128, (row + 1) * 128)
        rank = (within[row : row + 1, :] + above).astype(jnp.int32)
        ranks_ref[:, lanes] = jnp.where(mask[row : row + 1, :] > 0, rank, -1)
        batches_ref[:, lanes] = jnp.broadcast_to(batch[row : row + 1, :], (8, 128)).astype(jnp.bfloat16)
        above += jnp.sum(ones[row : row + 1, :], axis=1, keepdims=True)
    land_ref[0] = jnp.sum(ones).astype(jnp.int32)


def land_ranks(mask, batch):
    cols = mask.size
    return pl.pallas_call(
        ranks_kernel,
        in_specs=[pl.BlockSpec(memory_space=pltpu.VMEM)] * 2,
        out_specs=[pl.BlockSpec(memory_space=pltpu.VMEM)] * 2 + [pl.BlockSpec(memory_space=pltpu.SMEM)],
        out_shape=[shaped(jnp.int32, 1, cols), shaped(jnp.bfloat16, 8, cols), shaped(jnp.int32, 1)],
        compiler_params=pltpu.CompilerParams(vmem_limit_bytes=2**21),
        cost_estimate=pl.CostEstimate(flops=2**20, bytes_accessed=2**16, transcendentals=0),
        name="ranks",
    )(mask, batch)


def network(x, field, target, mask, batch, w_in, w_out, total, places):
    feats, cols = x.shape
    hid = w_out.shape[0]
    ranks, batch, land = land_ranks(mask, batch)
    table = jnp.asarray(ring_rows())
    f32, bf16 = jnp.float32, jnp.bfloat16
    tail = [2048, 2048, 2048, 2056, 2048, 2048]
    hbm = pl.BlockSpec(memory_space=pl.ANY)
    vmem = pl.BlockSpec(memory_space=pltpu.VMEM)
    smem = pl.BlockSpec(memory_space=pltpu.SMEM)
    new, *halves = pl.pallas_call(
        functools.partial(network_kernel, (BATCHES / (total * feats), total ** (-0.5))),
        in_specs=[smem, smem, hbm, hbm, hbm, hbm, hbm, vmem, vmem],
        out_specs=[hbm] * 7 + [vmem],
        scratch_shapes=[
            pltpu.VMEM((feats, cols), bf16),
            pltpu.VMEM((8, feats, 512), bf16),
            pltpu.VMEM((64, 2, 32, feats), bf16),
            pltpu.VMEM((feats, cols), bf16),
            pltpu.VMEM((feats, cols), f32),
            pltpu.VMEM((feats * 8, cols // 8), f32),
        ]
        + [pltpu.VMEM((size, 256), f32) for size in tail]
        + [
            pltpu.VMEM((64, 2, 32, cols), f32),
            pltpu.VMEM((64, 2, 32, cols), bf16),
            pltpu.VMEM((feats, cols), f32),
            pltpu.VMEM((cols, cols), bf16),
            pltpu.VMEM((feats, cols), bf16),
            pltpu.VMEM((cols, feats), bf16),
            pltpu.VMEM((feats, cols), bf16),
            pltpu.VMEM((cols, feats), bf16),
            pltpu.VMEM((1, cols), f32),
            pltpu.SemaphoreType.DMA((8,)),
            pltpu.SemaphoreType.DMA((8,)),
            pltpu.SemaphoreType.DMA((3,)),
            pltpu.SemaphoreType.DMA((7,)),
        ],
        out_shape=[shaped(f32, feats * 8, cols // 8)] + [shaped(f32, size, 256) for size in tail + [8]],
        compiler_params=pltpu.CompilerParams(vmem_limit_bytes=60 * 2**20),
        cost_estimate=pl.CostEstimate(
            flops=10 * cols * feats * hid, bytes_accessed=20 * 2**20, transcendentals=cols * hid
        ),
        name="network",
    )(land, table, x, w_in, w_out.reshape(64, 2, 32, feats), target, field, ranks, batch)
    streams = [[kept, lax.ppermute(sent, CORE, PAIR)] for kept, sent in zip(halves[:3], halves[3:6])]
    losses = halves[6] + streams[0][1][2048:]
    for stage in range(3):
        for turn in range(2):
            streams, losses = ring_round(streams, stage, turn, places, losses)
    grad_out = jnp.concatenate([part[:, :128] for (part,) in streams], axis=1)
    grad_in = jnp.concatenate([part[:, 128:] for (part,) in streams], axis=1)
    return new, grad_in, grad_out, losses[0, :BATCHES]


def on_device(state, target, land_mask, batch_map, diffusion, speed_x, speed_y, w_in, w_out):
    feats, rows_x, rows_y = state.shape
    field, x, strips = transported(state, diffusion, speed_x, speed_y)
    target, land_mask, batch_map, *_ = lax.optimization_barrier((target, land_mask, batch_map, *strips))
    local_cols = rows_x * rows_y
    total = local_cols * lax.axis_size(BX) * lax.axis_size(BY)
    new, grad_in, grad_out, batch_loss = network(
        x,
        field,
        target.reshape(feats, local_cols),
        land_mask,
        batch_map,
        w_in,
        w_out,
        total,
        ring_places(),
    )
    return (new.reshape(feats, rows_x, rows_y), grad_in, grad_out, batch_loss)


def solution(mesh):
    torus = Mesh(mesh.devices.reshape(2, 4, 4, 2, 2), BX + BY)
    return jax.shard_map(
        on_device,
        mesh=torus,
        in_specs=(P(None, BX, BY), P(None, BX, BY), P(BX, BY), P(BX, BY), P(), P(), P(), P(), P()),
        out_specs=(P(None, BX, BY), P(BX + BY, None), P(BX + BY, None), P()),
        check_vma=False,
    )
```

```python
import functools

import jax
import jax.numpy as jnp
import numpy as np
from jax import lax
from jax.experimental import pallas as pl
from jax.experimental.pallas import tpu as pltpu
from jax.sharding import Mesh
from jax.sharding import PartitionSpec as P

SUB = 3
BATCHES = 64
FEW = 640
FEW_ROWS = 32
BX = ("bx_0", "bx_1")
BY = ("by_0", "by_1", "by_2")
CORE = "by_2"
AXES = {"x": ("by_0", CORE), "y": ("bx_0", "by_1", CORE), "z": ("bx_1", CORE)}
ORDERS = ("xyz", "yzx", "zxy")
DIGITS = ((0, 3, 1, 2), (0, 1, 2, 3))
RING = {
    1: [(2 * p + c, 2 * (p ^ 1 if c == 0 else 3 - p) + c) for p in range(4) for c in range(2)],
    2: [(2 * p + c, 2 * (3 - p if c == 0 else p ^ 1) + c) for p in range(4) for c in range(2)],
}
PAIR = [(0, 1), (1, 0)]


def edge_kernel(state_ref, low_ref, high_ref, left_ref, right_ref):
    for row in range(8):
        cells = state_ref[pl.ds(row, 128, stride=8), :]
        if row < SUB:
            low_ref[0, row * 128 : (row + 1) * 128, :] = cells
        if row >= 8 - SUB:
            high_ref[0, (row - 8 + SUB) * 128 : (row - 7 + SUB) * 128, :] = cells
        turned = cells.T
        left_ref[0, row * 8 : (row + 1) * 8, :] = turned[:8, :]
        right_ref[0, row * 8 : (row + 1) * 8, :] = turned[120:, :]


def transport_kernel(
    state_ref, above_ref, below_ref, left_ref, right_ref,
    coef_0, coef_1, coef_2, coef_3, coef_4, field_ref, x_ref, even_ref, odd_ref,
):
    lane = lax.broadcasted_iota(jnp.int32, (128, 128), 1)
    gap = jnp.zeros((112, 128), jnp.float32)
    at_x, at_y = lax.axis_index(BX), lax.axis_index(BY)
    inside = [jnp.where(at_x > 0, 1.0, 0.0), jnp.where(at_x < lax.axis_size(BX) - 1, 1.0, 0.0)]
    beside = jnp.where(
        lane < 64, jnp.where(at_y < lax.axis_size(BY) - 1, 1.0, 0.0), jnp.where(at_y > 0, 1.0, 0.0)
    )
    for row in range(-SUB, 8 + SUB):
        if 0 <= row < 8:
            cells = state_ref[pl.ds(row, 128, stride=8), :]
            left, right = (ref[0, row * 8 : (row + 1) * 8, :] for ref in (left_ref, right_ref))
        else:
            far_ref, at = (above_ref, row + SUB) if row < 0 else (below_ref, row - 8)
            cells = far_ref[0, at * 128 : (at + 1) * 128, :]
            left, right = (
                far_ref[0, side + at * 8 : side + (at + 1) * 8, :]
                for side in (SUB * 128, SUB * 136)
            )
        even_ref[row + SUB, 0] = cells
        if -SUB < row < 7 + SUB:
            even_ref[row + SUB, 1] = jnp.concatenate([right, gap, left], axis=0).T
    lane = lane[:FEW_ROWS]
    beside = beside[:FEW_ROWS]

    @pl.loop(0, 128 // FEW_ROWS)
    def _(piece):
        feats = pl.ds(pl.multiple_of(piece * FEW_ROWS, FEW_ROWS), FEW_ROWS)
        centre, east, west, north, south = (ref[feats, :] for ref in (coef_0, coef_1, coef_2, coef_3, coef_4))
        here, there = even_ref, odd_ref
        for substep in range(SUB):
            margin = SUB - substep - 1
            for row in range(-margin, 8 + margin):
                at = row + SUB
                main, side = here[at, 0, feats, :], here[at, 1, feats, :]
                new = (
                    centre * main
                    + east * here[at + 1, 0, feats, :]
                    + west * here[at - 1, 0, feats, :]
                    + north * pltpu.roll(jnp.where(lane == 0, side, main), 127, 1)
                    + south * pltpu.roll(jnp.where(lane == 127, side, main), 1, 1)
                )
                if margin == 0:
                    field_ref[feats, row * 128 : (row + 1) * 128] = new
                    x_ref[feats, row * 128 : (row + 1) * 128] = new.astype(jnp.bfloat16)
                    continue
                outside = row < 0 or row > 7
                if outside:
                    new = new * inside[0 if row < 0 else 1]
                there[at, 0, feats, :] = new
                if not -margin < row < 7 + margin:
                    continue
                near = (
                    centre * side
                    + east * here[at + 1, 1, feats, :]
                    + west * here[at - 1, 1, feats, :]
                    + north * pltpu.roll(jnp.where(lane == 0, main, side), 127, 1)
                    + south * pltpu.roll(jnp.where(lane == 127, main, side), 1, 1)
                ) * beside
                if outside:
                    near = near * inside[0 if row < 0 else 1]
                there[at, 1, feats, :] = near
            here, there = there, here


def shifted(value, axis, step):
    count = lax.axis_size(axis)
    pairs = [(i, i + step) for i in range(count) if 0 <= i + step < count]
    return lax.ppermute(value, axis, pairs)


def transported(state, diffusion, speed_x, speed_y):
    feats = state.shape[0]
    f32 = jnp.float32
    flat = in_hbm(state.reshape(feats * 8, 128))
    chunk = lambda rows: pl.BlockSpec((1, rows, 128), lambda i: (i, 0, 0))
    low, high, left, right = pl.pallas_call(
        edge_kernel,
        grid=(feats // 128,),
        in_specs=[pl.BlockSpec((1024, 128), lambda i: (i, 0))],
        out_specs=[chunk(SUB * 144), chunk(SUB * 144), chunk(64), chunk(64)],
        out_shape=[shaped(f32, feats // 128, rows, 128) for rows in (SUB * 144, SUB * 144, 64, 64)],
        compiler_params=params(16),
        cost_estimate=pl.CostEstimate(flops=2**20, bytes_accessed=3 * 2**20, transcendentals=0),
        name="edges",
    )(flat)
    from_left = shifted(right, BY, 1)
    from_right = shifted(left, BY, -1)
    low, high = (
        lax.dynamic_update_slice(
            edge, jnp.concatenate([from_left[:, rows], from_right[:, rows]], axis=1), (0, SUB * 128, 0)
        )
        for edge, rows in ((low, slice(0, SUB * 8)), (high, slice((8 - SUB) * 8, 64)))
    )
    above = shifted(high, BX, 1)
    below = shifted(low, BX, -1)
    coefs = [
        jnp.broadcast_to(value[:, None], (feats, 128))
        for value in (
            1.0 - 4.0 * diffusion,
            diffusion - 0.5 * speed_x,
            diffusion + 0.5 * speed_x,
            diffusion - 0.5 * speed_y,
            diffusion + 0.5 * speed_y,
        )
    ]
    field, x = pl.pallas_call(
        transport_kernel,
        grid=(feats // 128,),
        in_specs=[
            pl.BlockSpec((1024, 128), lambda i: (i, 0)),
            chunk(SUB * 144),
            chunk(SUB * 144),
            chunk(64),
            chunk(64),
        ]
        + [pl.BlockSpec((128, 128), lambda i: (i, 0))] * 5,
        out_specs=[pl.BlockSpec((128, 1024), lambda i: (i, 0))] * 2,
        scratch_shapes=[pltpu.VMEM((14, 2, 128, 128), f32)] * 2,
        out_shape=[pltpu.HBM((feats, 1024), f32), pltpu.HBM((feats, 1024), jnp.bfloat16)],
        compiler_params=params(16),
        cost_estimate=pl.CostEstimate(flops=2**24, bytes_accessed=6 * 2**20, transcendentals=0),
        name="transport",
    )(flat, above, below, from_left, from_right, *coefs)
    return field, x, (from_left, from_right)


def position(axis):
    if axis == "y":
        return lax.axis_index("bx_0") * 2 + lax.axis_index("by_1")
    return lax.axis_index("by_0" if axis == "x" else "bx_1")


def ring_places():
    core = lax.axis_index(CORE)
    places = {}
    for axis in "xyz":
        at = position(axis)
        folded = jnp.where(at == 0, 0, jnp.where(at == 3, 1, at + 1))
        places[axis] = jnp.where(core == 0, folded, at)
    return places


def half_of(rows, size, bit):
    return lax.dynamic_slice_in_dim(rows, bit * size, size, 0)


def ring_turn(terms, axis, turn, places, riding=None):
    bit = places[axis] % 2 if turn else places[axis] // 2
    size = terms[0].shape[0] // 2
    leaving = sum(half_of(term, size, 1 - bit) for term in terms)
    if riding is not None:
        leaving = jnp.concatenate([leaving, riding], axis=0)
    coming = lax.ppermute(leaving, AXES[axis], RING[turn + 1])
    staying = sum(half_of(term, size, bit) for term in terms)
    return [staying + coming[:size]], (None if riding is None else riding + coming[size:])


def ring_round(streams, stage, turn, places, riding=None):
    moved = []
    for stream, order in enumerate(ORDERS):
        terms, carried = ring_turn(
            streams[stream], order[stage], turn, places, riding if stream == 0 else None
        )
        riding = carried if stream == 0 else riding
        moved.append(terms)
    return moved, riding


def ring_rows():
    table = np.zeros((2, len(ORDERS), 64), np.int32)
    for core in range(2):
        for block in range(64):
            y_hi, z, x, y_lo = block // 32, block // 8 % 4, block // 2 % 4, block % 2
            at = {"x": x, "y": 2 * y_hi + y_lo, "z": z}
            for stream, order in enumerate(ORDERS):
                spot = 0
                for axis in order:
                    spot = spot * 4 + DIGITS[core].index(at[axis])
                table[core, stream, block] = spot * 32
    return table.reshape(-1)


def by_width(scalar_ref, most, body):
    land = scalar_ref[0]
    pl.when(land <= FEW)(functools.partial(body, FEW))
    pl.when(land > FEW)(functools.partial(body, most))


ROWS = (((1,), (1,)), ((), ()))


def network_kernel(
    scale, scalar_ref, table_ref, x_hbm, win_hbm, wout_hbm, target_hbm, field_hbm, rank_ref, batch_ref,
    new_hbm, kept_hbm_a, kept_hbm_b, kept_hbm_c, sent_hbm_a, sent_hbm_b, sent_hbm_c, loss_ref,
    x_ref, win_ref, wout_ref, target_ref, field_ref, new_ref, kept_a, kept_b, kept_c, sent_a, sent_b, sent_c,
    slope_ref, hidden_ref, tend_ref, pick_ref, xc_ref, xn_ref, dtend_ref, dtn_ref, persq_ref,
    win_sem, wout_sem, in_sem, out_sem,
):
    feats, cols = x_ref.shape
    core = lax.axis_index(CORE)
    incoming = [
        pltpu.make_async_copy(source, ref, in_sem.at[k])
        for k, (source, ref) in enumerate(((x_hbm, x_ref), (target_hbm, target_ref), (field_hbm, field_ref)))
    ]
    outgoing = [
        pltpu.make_async_copy(ref, dest, out_sem.at[k])
        for k, (ref, dest) in enumerate(
            (
                (new_ref, new_hbm),
                (sent_a, sent_hbm_a),
                (sent_b, sent_hbm_b),
                (sent_c, sent_hbm_c),
                (kept_a, kept_hbm_a),
                (kept_b, kept_hbm_b),
                (kept_c, kept_hbm_c),
            )
        )
    ]

    def win_copy(piece):
        return pltpu.make_async_copy(
            win_hbm.at[:, pl.ds(pl.multiple_of(piece * 512, 512), 512)], win_ref.at[piece], win_sem.at[piece]
        )

    def wout_copy(piece):
        at = pl.ds(piece * 8, 8)
        return pltpu.make_async_copy(wout_hbm.at[at], wout_ref.at[at], wout_sem.at[piece])

    incoming[0].start()
    for piece in range(8):
        win_copy(piece).start()
        wout_copy(piece).start()
    incoming[1].start()
    incoming[2].start()

    def run(n):
        @pl.loop(0, n // 128)
        def _(block):
            slot = lax.broadcasted_iota(jnp.int32, (128, cols), 0) + block * 128
            pick_ref[pl.ds(pl.multiple_of(block * 128, 128), 128), :] = jnp.where(
                slot == rank_ref[...], 1.0, 0.0
            ).astype(jnp.bfloat16)

        incoming[0].wait()

        @pl.loop(0, feats // 128)
        def _(block):
            some = pl.ds(pl.multiple_of(block * 128, 128), 128)
            packed = lax.dot_general(x_ref[some, :], pick_ref[:n, :], ROWS, preferred_element_type=jnp.float32)
            packed = packed.astype(jnp.bfloat16)
            xc_ref[some, :n] = packed
            xn_ref[:n, some] = packed.T
            tend_ref[some, :n] = jnp.zeros((128, n), jnp.float32)

        def activate(piece):
            for part in range(2):
                rows = slice(part * 256, (part + 1) * 256)
                pre = jnp.dot(win_ref[piece, :, rows].T, xc_ref[:, :n], preferred_element_type=jnp.float32)
                sig = 0.5 * jnp.tanh(0.5 * pre) + 0.5
                act = pre * sig
                at = pl.ds(piece * 8 + part * 4, 4)
                slope_ref[at, :, :, :n] = (sig + act * (1.0 - sig)).reshape(4, 2, 32, n)
                hidden_ref[at, :, :, :n] = act.astype(jnp.bfloat16).reshape(4, 2, 32, n)

        def project(piece):
            at = pl.ds(piece * 8, 8)
            tend_ref[:, :n] += jnp.dot(
                wout_ref[at].reshape(512, feats).T,
                hidden_ref[at, :, :, :n].reshape(512, n),
                preferred_element_type=jnp.float32,
            )

        win_copy(0).wait()
        activate(0)

        @pl.loop(1, 8)
        def _(piece):
            win_copy(piece).wait()
            wout_copy(piece - 1).wait()
            project(piece - 1)
            activate(piece)

        wout_copy(7).wait()
        project(7)
        pick = pick_ref[:n, :]
        persq_ref[:, :n] = jnp.zeros((1, n), jnp.float32)
        incoming[1].wait()
        incoming[2].wait()

        @pl.loop(0, feats // 128)
        def _(block):
            some = pl.ds(pl.multiple_of(block * 128, 128), 128)
            tend = tend_ref[some, :n]
            wanted = lax.dot_general(target_ref[some, :], pick_ref[:n, :], ROWS, preferred_element_type=jnp.float32)
            err = tend - wanted
            persq_ref[:, :n] += 0.5 * jnp.sum(err * err, axis=0, keepdims=True)
            dtend = (err * scale[1]).astype(jnp.bfloat16)
            dtend_ref[some, :n] = dtend
            dtn_ref[:n, some] = dtend.T
            coarse = tend.astype(jnp.bfloat16)
            fine = (tend - coarse.astype(jnp.float32)).astype(jnp.bfloat16)
            spread = jnp.dot(coarse, pick_ref[:n, :], preferred_element_type=jnp.float32)
            spread += jnp.dot(fine, pick_ref[:n, :], preferred_element_type=jnp.float32)
            new = field_ref[some, :] + 0.5 * spread
            for row in range(8):
                new_ref[pl.ds(block * 1024 + row, 128, stride=8), :] = new[:, row * 128 : (row + 1) * 128]

        outgoing[0].start()
        persq = persq_ref[:, :n]
        batch = lax.dot_general(batch_ref[...], pick, ROWS, preferred_element_type=jnp.float32)
        which = lax.broadcasted_iota(jnp.int32, (128, n), 0).astype(jnp.float32)
        onehot = jnp.where(which == batch[0:1, :], 1.0, 0.0)
        loss = scale[0] * lax.dot_general(
            jnp.broadcast_to(persq, (8, n)),
            onehot,
            ROWS,
            precision=lax.Precision.HIGHEST,
            preferred_element_type=jnp.float32,
        )
        for side in (0, 128):
            sent_a[2048:, side : side + 128] = loss
            loss_ref[:, side : side + 128] = loss

        for digit, out_refs, copies in (
            (1 - core, (sent_a, sent_b, sent_c), outgoing[1:4]),
            (core, (kept_a, kept_b, kept_c), outgoing[4:]),
        ):

            @pl.loop(0, 4)
            def _(piece, digit=digit, out_refs=out_refs):
                at = pl.ds(piece * 16, 16)
                dhid = jnp.dot(
                    wout_ref[at, digit].reshape(512, feats), dtend_ref[:, :n], preferred_element_type=jnp.float32
                )
                dpre = (dhid * slope_ref[at, digit, :, :n].reshape(512, n)).astype(jnp.bfloat16)
                sums = (
                    jnp.dot(
                        hidden_ref[at, digit, :, :n].reshape(512, n), dtn_ref[:n, :], preferred_element_type=jnp.float32
                    ),
                    jnp.dot(dpre, xn_ref[:n, :], preferred_element_type=jnp.float32),
                )
                for block in range(16):
                    for stream in range(3):
                        row = table_ref[digit * 192 + stream * 64 + piece * 16 + block]
                        for which in range(2):
                            out_refs[stream][
                                pl.ds(pl.multiple_of(row, 32), 32), which * 128 : (which + 1) * 128
                            ] = sums[which][block * 32 : (block + 1) * 32, stream * 128 : (stream + 1) * 128]

            for copy in copies:
                copy.start()

    by_width(scalar_ref, cols, run)
    for copy in outgoing:
        copy.wait()


def in_hbm(value):
    return pltpu.with_memory_space_constraint(value, pltpu.HBM)


def whole(*shape):
    return pl.BlockSpec(shape, lambda i, *_: (0,) * len(shape), pipeline_mode=pl.Buffered(1))


def shaped(dtype, *shape):
    return jax.ShapeDtypeStruct(shape, dtype)


def params(megabytes):
    return pltpu.CompilerParams(dimension_semantics=("arbitrary",), vmem_limit_bytes=megabytes * 2**20)


def ranks_kernel(mask_ref, batch_ref, ranks_ref, batches_ref, land_ref):
    mask = mask_ref[...]
    ones = mask.astype(jnp.float32)
    first = lax.broadcasted_iota(jnp.int32, (128, 128), 0) < lax.broadcasted_iota(jnp.int32, (128, 128), 1)
    before = jnp.where(first, 1.0, 0.0).astype(jnp.bfloat16)
    within = jnp.dot(ones.astype(jnp.bfloat16), before, preferred_element_type=jnp.float32)
    batch = batch_ref[...].astype(jnp.float32)
    above = jnp.zeros((1, 1), jnp.float32)
    for row in range(8):
        lanes = slice(row * 128, (row + 1) * 128)
        rank = (within[row : row + 1, :] + above).astype(jnp.int32)
        ranks_ref[:, lanes] = jnp.where(mask[row : row + 1, :] > 0, rank, -1)
        batches_ref[:, lanes] = jnp.broadcast_to(batch[row : row + 1, :], (8, 128)).astype(jnp.bfloat16)
        above += jnp.sum(ones[row : row + 1, :], axis=1, keepdims=True)
    land_ref[0] = jnp.sum(ones).astype(jnp.int32)


def land_ranks(mask, batch):
    cols = mask.size
    return pl.pallas_call(
        ranks_kernel,
        in_specs=[pl.BlockSpec(memory_space=pltpu.VMEM)] * 2,
        out_specs=[pl.BlockSpec(memory_space=pltpu.VMEM)] * 2 + [pl.BlockSpec(memory_space=pltpu.SMEM)],
        out_shape=[shaped(jnp.int32, 1, cols), shaped(jnp.bfloat16, 8, cols), shaped(jnp.int32, 1)],
        compiler_params=pltpu.CompilerParams(vmem_limit_bytes=2**21),
        cost_estimate=pl.CostEstimate(flops=2**20, bytes_accessed=2**16, transcendentals=0),
        name="ranks",
    )(mask, batch)


def network(x, field, target, mask, batch, w_in, w_out, total, places):
    feats, cols = x.shape
    hid = w_out.shape[0]
    ranks, batch, land = land_ranks(mask, batch)
    table = jnp.asarray(ring_rows())
    f32, bf16 = jnp.float32, jnp.bfloat16
    tail = [2048, 2048, 2048, 2056, 2048, 2048]
    hbm = pl.BlockSpec(memory_space=pl.ANY)
    vmem = pl.BlockSpec(memory_space=pltpu.VMEM)
    smem = pl.BlockSpec(memory_space=pltpu.SMEM)
    new, *halves = pl.pallas_call(
        functools.partial(network_kernel, (BATCHES / (total * feats), total ** (-0.5))),
        in_specs=[smem, smem, hbm, hbm, hbm, hbm, hbm, vmem, vmem],
        out_specs=[hbm] * 7 + [vmem],
        scratch_shapes=[
            pltpu.VMEM((feats, cols), bf16),
            pltpu.VMEM((8, feats, 512), bf16),
            pltpu.VMEM((64, 2, 32, feats), bf16),
            pltpu.VMEM((feats, cols), bf16),
            pltpu.VMEM((feats, cols), f32),
            pltpu.VMEM((feats * 8, cols // 8), f32),
        ]
        + [pltpu.VMEM((size, 256), f32) for size in tail]
        + [
            pltpu.VMEM((64, 2, 32, cols), f32),
            pltpu.VMEM((64, 2, 32, cols), bf16),
            pltpu.VMEM((feats, cols), f32),
            pltpu.VMEM((cols, cols), bf16),
            pltpu.VMEM((feats, cols), bf16),
            pltpu.VMEM((cols, feats), bf16),
            pltpu.VMEM((feats, cols), bf16),
            pltpu.VMEM((cols, feats), bf16),
            pltpu.VMEM((1, cols), f32),
            pltpu.SemaphoreType.DMA((8,)),
            pltpu.SemaphoreType.DMA((8,)),
            pltpu.SemaphoreType.DMA((3,)),
            pltpu.SemaphoreType.DMA((7,)),
        ],
        out_shape=[shaped(f32, feats * 8, cols // 8)] + [shaped(f32, size, 256) for size in tail + [8]],
        compiler_params=pltpu.CompilerParams(vmem_limit_bytes=60 * 2**20),
        cost_estimate=pl.CostEstimate(
            flops=10 * cols * feats * hid, bytes_accessed=20 * 2**20, transcendentals=cols * hid
        ),
        name="network",
    )(land, table, x, w_in, w_out.reshape(64, 2, 32, feats), target, field, ranks, batch)
    streams = [[kept, lax.ppermute(sent, CORE, PAIR)] for kept, sent in zip(halves[:3], halves[3:6])]
    losses = halves[6] + streams[0][1][2048:]
    for stage in range(3):
        for turn in range(2):
            streams, losses = ring_round(streams, stage, turn, places, losses)
    grad_out = jnp.concatenate([part[:, :128] for (part,) in streams], axis=1)
    grad_in = jnp.concatenate([part[:, 128:] for (part,) in streams], axis=1)
    return new, grad_in, grad_out, losses[0, :BATCHES]


def on_device(state, target, land_mask, batch_map, diffusion, speed_x, speed_y, w_in, w_out):
    feats, rows_x, rows_y = state.shape
    field, x, strips = transported(state, diffusion, speed_x, speed_y)
    target, land_mask, batch_map, *_ = lax.optimization_barrier((target, land_mask, batch_map, *strips))
    local_cols = rows_x * rows_y
    total = local_cols * lax.axis_size(BX) * lax.axis_size(BY)
    new, grad_in, grad_out, batch_loss = network(
        x,
        field,
        target.reshape(feats, local_cols),
        land_mask,
        batch_map,
        w_in,
        w_out,
        total,
        ring_places(),
    )
    return (new.reshape(feats, rows_x, rows_y), grad_in, grad_out, batch_loss)


def solution(mesh):
    torus = Mesh(mesh.devices.reshape(2, 4, 4, 2, 2), BX + BY)
    return jax.shard_map(
        on_device,
        mesh=torus,
        in_specs=(P(None, BX, BY), P(None, BX, BY), P(BX, BY), P(BX, BY), P(), P(), P(), P(), P()),
        out_specs=(P(None, BX, BY), P(BX + BY, None), P(BX + BY, None), P()),
        check_vma=False,
    )
```

```python
import functools

import jax
import jax.numpy as jnp
import numpy as np
from jax import lax
from jax.experimental import pallas as pl
from jax.experimental.pallas import tpu as pltpu
from jax.sharding import Mesh
from jax.sharding import PartitionSpec as P

SUB = 3
BATCHES = 64
FEW = 640
FEW_ROWS = 64
BX = ("bx_0", "bx_1")
BY = ("by_0", "by_1", "by_2")
CORE = "by_2"
AXES = {"x": ("by_0", CORE), "y": ("bx_0", "by_1", CORE), "z": ("bx_1", CORE)}
ORDERS = ("xyz", "yzx", "zxy")
DIGITS = ((0, 3, 1, 2), (0, 1, 2, 3))
RING = {
    1: [(2 * p + c, 2 * (p ^ 1 if c == 0 else 3 - p) + c) for p in range(4) for c in range(2)],
    2: [(2 * p + c, 2 * (3 - p if c == 0 else p ^ 1) + c) for p in range(4) for c in range(2)],
}
PAIR = [(0, 1), (1, 0)]


def edge_kernel(state_ref, low_ref, high_ref, left_ref, right_ref):
    for row in range(8):
        cells = state_ref[pl.ds(row, 128, stride=8), :]
        if row < SUB:
            low_ref[0, row * 128 : (row + 1) * 128, :] = cells
        if row >= 8 - SUB:
            high_ref[0, (row - 8 + SUB) * 128 : (row - 7 + SUB) * 128, :] = cells
        turned = cells.T
        left_ref[0, row * 8 : (row + 1) * 8, :] = turned[:8, :]
        right_ref[0, row * 8 : (row + 1) * 8, :] = turned[120:, :]


def transport_kernel(
    state_ref, above_ref, below_ref, left_ref, right_ref,
    coef_0, coef_1, coef_2, coef_3, coef_4, field_ref, x_ref, even_ref, odd_ref,
):
    lane = lax.broadcasted_iota(jnp.int32, (128, 128), 1)
    gap = jnp.zeros((112, 128), jnp.float32)
    at_x, at_y = lax.axis_index(BX), lax.axis_index(BY)
    inside = [jnp.where(at_x > 0, 1.0, 0.0), jnp.where(at_x < lax.axis_size(BX) - 1, 1.0, 0.0)]
    beside = jnp.where(
        lane < 64, jnp.where(at_y < lax.axis_size(BY) - 1, 1.0, 0.0), jnp.where(at_y > 0, 1.0, 0.0)
    )
    for row in range(-SUB, 8 + SUB):
        if 0 <= row < 8:
            cells = state_ref[pl.ds(row, 128, stride=8), :]
            left, right = (ref[0, row * 8 : (row + 1) * 8, :] for ref in (left_ref, right_ref))
        else:
            far_ref, at = (above_ref, row + SUB) if row < 0 else (below_ref, row - 8)
            cells = far_ref[0, at * 128 : (at + 1) * 128, :]
            left, right = (
                far_ref[0, side + at * 8 : side + (at + 1) * 8, :]
                for side in (SUB * 128, SUB * 136)
            )
        even_ref[row + SUB, 0] = cells
        if -SUB < row < 7 + SUB:
            even_ref[row + SUB, 1] = jnp.concatenate([right, gap, left], axis=0).T
    lane = lane[:FEW_ROWS]
    beside = beside[:FEW_ROWS]

    @pl.loop(0, 128 // FEW_ROWS)
    def _(piece):
        feats = pl.ds(pl.multiple_of(piece * FEW_ROWS, FEW_ROWS), FEW_ROWS)
        centre, east, west, north, south = (ref[feats, :] for ref in (coef_0, coef_1, coef_2, coef_3, coef_4))
        here, there = even_ref, odd_ref
        for substep in range(SUB):
            margin = SUB - substep - 1
            for row in range(-margin, 8 + margin):
                at = row + SUB
                main, side = here[at, 0, feats, :], here[at, 1, feats, :]
                new = (
                    centre * main
                    + east * here[at + 1, 0, feats, :]
                    + west * here[at - 1, 0, feats, :]
                    + north * pltpu.roll(jnp.where(lane == 0, side, main), 127, 1)
                    + south * pltpu.roll(jnp.where(lane == 127, side, main), 1, 1)
                )
                if margin == 0:
                    field_ref[feats, row * 128 : (row + 1) * 128] = new
                    x_ref[feats, row * 128 : (row + 1) * 128] = new.astype(jnp.bfloat16)
                    continue
                outside = row < 0 or row > 7
                if outside:
                    new = new * inside[0 if row < 0 else 1]
                there[at, 0, feats, :] = new
                if not -margin < row < 7 + margin:
                    continue
                near = (
                    centre * side
                    + east * here[at + 1, 1, feats, :]
                    + west * here[at - 1, 1, feats, :]
                    + north * pltpu.roll(jnp.where(lane == 0, main, side), 127, 1)
                    + south * pltpu.roll(jnp.where(lane == 127, main, side), 1, 1)
                ) * beside
                if outside:
                    near = near * inside[0 if row < 0 else 1]
                there[at, 1, feats, :] = near
            here, there = there, here


def shifted(value, axis, step):
    count = lax.axis_size(axis)
    pairs = [(i, i + step) for i in range(count) if 0 <= i + step < count]
    return lax.ppermute(value, axis, pairs)


def transported(state, diffusion, speed_x, speed_y):
    feats = state.shape[0]
    f32 = jnp.float32
    flat = in_hbm(state.reshape(feats * 8, 128))
    chunk = lambda rows: pl.BlockSpec((1, rows, 128), lambda i: (i, 0, 0))
    low, high, left, right = pl.pallas_call(
        edge_kernel,
        grid=(feats // 128,),
        in_specs=[pl.BlockSpec((1024, 128), lambda i: (i, 0))],
        out_specs=[chunk(SUB * 144), chunk(SUB * 144), chunk(64), chunk(64)],
        out_shape=[shaped(f32, feats // 128, rows, 128) for rows in (SUB * 144, SUB * 144, 64, 64)],
        compiler_params=params(16),
        cost_estimate=pl.CostEstimate(flops=2**20, bytes_accessed=3 * 2**20, transcendentals=0),
        name="edges",
    )(flat)
    from_left = shifted(right, BY, 1)
    from_right = shifted(left, BY, -1)
    low, high = (
        lax.dynamic_update_slice(
            edge, jnp.concatenate([from_left[:, rows], from_right[:, rows]], axis=1), (0, SUB * 128, 0)
        )
        for edge, rows in ((low, slice(0, SUB * 8)), (high, slice((8 - SUB) * 8, 64)))
    )
    above = shifted(high, BX, 1)
    below = shifted(low, BX, -1)
    coefs = [
        jnp.broadcast_to(value[:, None], (feats, 128))
        for value in (
            1.0 - 4.0 * diffusion,
            diffusion - 0.5 * speed_x,
            diffusion + 0.5 * speed_x,
            diffusion - 0.5 * speed_y,
            diffusion + 0.5 * speed_y,
        )
    ]
    field, x = pl.pallas_call(
        transport_kernel,
        grid=(feats // 128,),
        in_specs=[
            pl.BlockSpec((1024, 128), lambda i: (i, 0)),
            chunk(SUB * 144),
            chunk(SUB * 144),
            chunk(64),
            chunk(64),
        ]
        + [pl.BlockSpec((128, 128), lambda i: (i, 0))] * 5,
        out_specs=[pl.BlockSpec((128, 1024), lambda i: (i, 0))] * 2,
        scratch_shapes=[pltpu.VMEM((14, 2, 128, 128), f32)] * 2,
        out_shape=[pltpu.HBM((feats, 1024), f32), pltpu.HBM((feats, 1024), jnp.bfloat16)],
        compiler_params=params(16),
        cost_estimate=pl.CostEstimate(flops=2**24, bytes_accessed=6 * 2**20, transcendentals=0),
        name="transport",
    )(flat, above, below, from_left, from_right, *coefs)
    return field, x, (from_left, from_right)


def position(axis):
    if axis == "y":
        return lax.axis_index("bx_0") * 2 + lax.axis_index("by_1")
    return lax.axis_index("by_0" if axis == "x" else "bx_1")


def ring_places():
    core = lax.axis_index(CORE)
    places = {}
    for axis in "xyz":
        at = position(axis)
        folded = jnp.where(at == 0, 0, jnp.where(at == 3, 1, at + 1))
        places[axis] = jnp.where(core == 0, folded, at)
    return places


def half_of(rows, size, bit):
    return lax.dynamic_slice_in_dim(rows, bit * size, size, 0)


def ring_turn(terms, axis, turn, places, riding=None):
    bit = places[axis] % 2 if turn else places[axis] // 2
    size = terms[0].shape[0] // 2
    leaving = sum(half_of(term, size, 1 - bit) for term in terms)
    if riding is not None:
        leaving = jnp.concatenate([leaving, riding], axis=0)
    coming = lax.ppermute(leaving, AXES[axis], RING[turn + 1])
    staying = sum(half_of(term, size, bit) for term in terms)
    return [staying + coming[:size]], (None if riding is None else riding + coming[size:])


def ring_round(streams, stage, turn, places, riding=None):
    moved = []
    for stream, order in enumerate(ORDERS):
        terms, carried = ring_turn(
            streams[stream], order[stage], turn, places, riding if stream == 0 else None
        )
        riding = carried if stream == 0 else riding
        moved.append(terms)
    return moved, riding


def ring_rows():
    table = np.zeros((2, len(ORDERS), 64), np.int32)
    for core in range(2):
        for block in range(64):
            y_hi, z, x, y_lo = block // 32, block // 8 % 4, block // 2 % 4, block % 2
            at = {"x": x, "y": 2 * y_hi + y_lo, "z": z}
            for stream, order in enumerate(ORDERS):
                spot = 0
                for axis in order:
                    spot = spot * 4 + DIGITS[core].index(at[axis])
                table[core, stream, block] = spot * 32
    return table.reshape(-1)


def by_width(scalar_ref, most, body):
    land = scalar_ref[0]
    pl.when(land <= FEW)(functools.partial(body, FEW))
    pl.when(land > FEW)(functools.partial(body, most))


ROWS = (((1,), (1,)), ((), ()))


def network_kernel(
    scale, scalar_ref, table_ref, x_hbm, win_hbm, wout_hbm, target_hbm, field_hbm, rank_ref, batch_ref,
    new_hbm, kept_hbm_a, kept_hbm_b, kept_hbm_c, sent_hbm_a, sent_hbm_b, sent_hbm_c, loss_ref,
    x_ref, win_ref, wout_ref, target_ref, field_ref, new_ref, kept_a, kept_b, kept_c, sent_a, sent_b, sent_c,
    slope_ref, hidden_ref, tend_ref, pick_ref, xc_ref, xn_ref, dtend_ref, dtn_ref, persq_ref,
    win_sem, wout_sem, in_sem, out_sem,
):
    feats, cols = x_ref.shape
    core = lax.axis_index(CORE)
    incoming = [
        pltpu.make_async_copy(source, ref, in_sem.at[k])
        for k, (source, ref) in enumerate(((x_hbm, x_ref), (target_hbm, target_ref), (field_hbm, field_ref)))
    ]
    outgoing = [
        pltpu.make_async_copy(ref, dest, out_sem.at[k])
        for k, (ref, dest) in enumerate(
            (
                (new_ref, new_hbm),
                (sent_a, sent_hbm_a),
                (sent_b, sent_hbm_b),
                (sent_c, sent_hbm_c),
                (kept_a, kept_hbm_a),
                (kept_b, kept_hbm_b),
                (kept_c, kept_hbm_c),
            )
        )
    ]

    def win_copy(piece):
        return pltpu.make_async_copy(
            win_hbm.at[:, pl.ds(pl.multiple_of(piece * 512, 512), 512)], win_ref.at[piece], win_sem.at[piece]
        )

    def wout_copy(piece):
        at = pl.ds(piece * 8, 8)
        return pltpu.make_async_copy(wout_hbm.at[at], wout_ref.at[at], wout_sem.at[piece])

    incoming[0].start()
    for piece in range(8):
        win_copy(piece).start()
        wout_copy(piece).start()
    incoming[1].start()
    incoming[2].start()

    def run(n):
        @pl.loop(0, n // 128)
        def _(block):
            slot = lax.broadcasted_iota(jnp.int32, (128, cols), 0) + block * 128
            pick_ref[pl.ds(pl.multiple_of(block * 128, 128), 128), :] = jnp.where(
                slot == rank_ref[...], 1.0, 0.0
            ).astype(jnp.bfloat16)

        incoming[0].wait()

        @pl.loop(0, feats // 128)
        def _(block):
            some = pl.ds(pl.multiple_of(block * 128, 128), 128)
            packed = lax.dot_general(x_ref[some, :], pick_ref[:n, :], ROWS, preferred_element_type=jnp.float32)
            packed = packed.astype(jnp.bfloat16)
            xc_ref[some, :n] = packed
            xn_ref[:n, some] = packed.T
            tend_ref[some, :n] = jnp.zeros((128, n), jnp.float32)

        def activate(piece):
            for part in range(2):
                rows = slice(part * 256, (part + 1) * 256)
                pre = jnp.dot(win_ref[piece, :, rows].T, xc_ref[:, :n], preferred_element_type=jnp.float32)
                sig = 0.5 * jnp.tanh(0.5 * pre) + 0.5
                act = pre * sig
                at = pl.ds(piece * 8 + part * 4, 4)
                slope_ref[at, :, :, :n] = (sig + act * (1.0 - sig)).reshape(4, 2, 32, n)
                hidden_ref[at, :, :, :n] = act.astype(jnp.bfloat16).reshape(4, 2, 32, n)

        def project(piece):
            at = pl.ds(piece * 8, 8)
            tend_ref[:, :n] += jnp.dot(
                wout_ref[at].reshape(512, feats).T,
                hidden_ref[at, :, :, :n].reshape(512, n),
                preferred_element_type=jnp.float32,
            )

        win_copy(0).wait()
        activate(0)

        @pl.loop(1, 8)
        def _(piece):
            win_copy(piece).wait()
            wout_copy(piece - 1).wait()
            project(piece - 1)
            activate(piece)

        wout_copy(7).wait()
        project(7)
        pick = pick_ref[:n, :]
        persq_ref[:, :n] = jnp.zeros((1, n), jnp.float32)
        incoming[1].wait()
        incoming[2].wait()

        @pl.loop(0, feats // 128)
        def _(block):
            some = pl.ds(pl.multiple_of(block * 128, 128), 128)
            tend = tend_ref[some, :n]
            wanted = lax.dot_general(target_ref[some, :], pick_ref[:n, :], ROWS, preferred_element_type=jnp.float32)
            err = tend - wanted
            persq_ref[:, :n] += 0.5 * jnp.sum(err * err, axis=0, keepdims=True)
            dtend = (err * scale[1]).astype(jnp.bfloat16)
            dtend_ref[some, :n] = dtend
            dtn_ref[:n, some] = dtend.T
            coarse = tend.astype(jnp.bfloat16)
            fine = (tend - coarse.astype(jnp.float32)).astype(jnp.bfloat16)
            spread = jnp.dot(coarse, pick_ref[:n, :], preferred_element_type=jnp.float32)
            spread += jnp.dot(fine, pick_ref[:n, :], preferred_element_type=jnp.float32)
            new = field_ref[some, :] + 0.5 * spread
            for row in range(8):
                new_ref[pl.ds(block * 1024 + row, 128, stride=8), :] = new[:, row * 128 : (row + 1) * 128]

        outgoing[0].start()
        persq = persq_ref[:, :n]
        batch = lax.dot_general(batch_ref[...], pick, ROWS, preferred_element_type=jnp.float32)
        which = lax.broadcasted_iota(jnp.int32, (128, n), 0).astype(jnp.float32)
        onehot = jnp.where(which == batch[0:1, :], 1.0, 0.0)
        loss = scale[0] * lax.dot_general(
            jnp.broadcast_to(persq, (8, n)),
            onehot,
            ROWS,
            precision=lax.Precision.HIGHEST,
            preferred_element_type=jnp.float32,
        )
        for side in (0, 128):
            sent_a[2048:, side : side + 128] = loss
            loss_ref[:, side : side + 128] = loss

        for digit, out_refs, copies in (
            (1 - core, (sent_a, sent_b, sent_c), outgoing[1:4]),
            (core, (kept_a, kept_b, kept_c), outgoing[4:]),
        ):

            @pl.loop(0, 4)
            def _(piece, digit=digit, out_refs=out_refs):
                at = pl.ds(piece * 16, 16)
                dhid = jnp.dot(
                    wout_ref[at, digit].reshape(512, feats), dtend_ref[:, :n], preferred_element_type=jnp.float32
                )
                dpre = (dhid * slope_ref[at, digit, :, :n].reshape(512, n)).astype(jnp.bfloat16)
                sums = (
                    jnp.dot(
                        hidden_ref[at, digit, :, :n].reshape(512, n), dtn_ref[:n, :], preferred_element_type=jnp.float32
                    ),
                    jnp.dot(dpre, xn_ref[:n, :], preferred_element_type=jnp.float32),
                )
                for block in range(16):
                    for stream in range(3):
                        row = table_ref[digit * 192 + stream * 64 + piece * 16 + block]
                        for which in range(2):
                            out_refs[stream][
                                pl.ds(pl.multiple_of(row, 32), 32), which * 128 : (which + 1) * 128
                            ] = sums[which][block * 32 : (block + 1) * 32, stream * 128 : (stream + 1) * 128]

            for copy in copies:
                copy.start()

    by_width(scalar_ref, cols, run)
    for copy in outgoing:
        copy.wait()


def in_hbm(value):
    return pltpu.with_memory_space_constraint(value, pltpu.HBM)


def whole(*shape):
    return pl.BlockSpec(shape, lambda i, *_: (0,) * len(shape), pipeline_mode=pl.Buffered(1))


def shaped(dtype, *shape):
    return jax.ShapeDtypeStruct(shape, dtype)


def params(megabytes):
    return pltpu.CompilerParams(dimension_semantics=("arbitrary",), vmem_limit_bytes=megabytes * 2**20)


def ranks_kernel(mask_ref, batch_ref, ranks_ref, batches_ref, land_ref):
    mask = mask_ref[...]
    ones = mask.astype(jnp.float32)
    first = lax.broadcasted_iota(jnp.int32, (128, 128), 0) < lax.broadcasted_iota(jnp.int32, (128, 128), 1)
    before = jnp.where(first, 1.0, 0.0).astype(jnp.bfloat16)
    within = jnp.dot(ones.astype(jnp.bfloat16), before, preferred_element_type=jnp.float32)
    batch = batch_ref[...].astype(jnp.float32)
    above = jnp.zeros((1, 1), jnp.float32)
    for row in range(8):
        lanes = slice(row * 128, (row + 1) * 128)
        rank = (within[row : row + 1, :] + above).astype(jnp.int32)
        ranks_ref[:, lanes] = jnp.where(mask[row : row + 1, :] > 0, rank, -1)
        batches_ref[:, lanes] = jnp.broadcast_to(batch[row : row + 1, :], (8, 128)).astype(jnp.bfloat16)
        above += jnp.sum(ones[row : row + 1, :], axis=1, keepdims=True)
    land_ref[0] = jnp.sum(ones).astype(jnp.int32)


def land_ranks(mask, batch):
    cols = mask.size
    return pl.pallas_call(
        ranks_kernel,
        in_specs=[pl.BlockSpec(memory_space=pltpu.VMEM)] * 2,
        out_specs=[pl.BlockSpec(memory_space=pltpu.VMEM)] * 2 + [pl.BlockSpec(memory_space=pltpu.SMEM)],
        out_shape=[shaped(jnp.int32, 1, cols), shaped(jnp.bfloat16, 8, cols), shaped(jnp.int32, 1)],
        compiler_params=pltpu.CompilerParams(vmem_limit_bytes=2**21),
        cost_estimate=pl.CostEstimate(flops=2**20, bytes_accessed=2**16, transcendentals=0),
        name="ranks",
    )(mask, batch)


def network(x, field, target, mask, batch, w_in, w_out, total, places):
    feats, cols = x.shape
    hid = w_out.shape[0]
    ranks, batch, land = land_ranks(mask, batch)
    table = jnp.asarray(ring_rows())
    f32, bf16 = jnp.float32, jnp.bfloat16
    tail = [2048, 2048, 2048, 2056, 2048, 2048]
    hbm = pl.BlockSpec(memory_space=pl.ANY)
    vmem = pl.BlockSpec(memory_space=pltpu.VMEM)
    smem = pl.BlockSpec(memory_space=pltpu.SMEM)
    new, *halves = pl.pallas_call(
        functools.partial(network_kernel, (BATCHES / (total * feats), total ** (-0.5))),
        in_specs=[smem, smem, hbm, hbm, hbm, hbm, hbm, vmem, vmem],
        out_specs=[hbm] * 7 + [vmem],
        scratch_shapes=[
            pltpu.VMEM((feats, cols), bf16),
            pltpu.VMEM((8, feats, 512), bf16),
            pltpu.VMEM((64, 2, 32, feats), bf16),
            pltpu.VMEM((feats, cols), bf16),
            pltpu.VMEM((feats, cols), f32),
            pltpu.VMEM((feats * 8, cols // 8), f32),
        ]
        + [pltpu.VMEM((size, 256), f32) for size in tail]
        + [
            pltpu.VMEM((64, 2, 32, cols), f32),
            pltpu.VMEM((64, 2, 32, cols), bf16),
            pltpu.VMEM((feats, cols), f32),
            pltpu.VMEM((cols, cols), bf16),
            pltpu.VMEM((feats, cols), bf16),
            pltpu.VMEM((cols, feats), bf16),
            pltpu.VMEM((feats, cols), bf16),
            pltpu.VMEM((cols, feats), bf16),
            pltpu.VMEM((1, cols), f32),
            pltpu.SemaphoreType.DMA((8,)),
            pltpu.SemaphoreType.DMA((8,)),
            pltpu.SemaphoreType.DMA((3,)),
            pltpu.SemaphoreType.DMA((7,)),
        ],
        out_shape=[shaped(f32, feats * 8, cols // 8)] + [shaped(f32, size, 256) for size in tail + [8]],
        compiler_params=pltpu.CompilerParams(vmem_limit_bytes=60 * 2**20),
        cost_estimate=pl.CostEstimate(
            flops=10 * cols * feats * hid, bytes_accessed=20 * 2**20, transcendentals=cols * hid
        ),
        name="network",
    )(land, table, x, w_in, w_out.reshape(64, 2, 32, feats), target, field, ranks, batch)
    streams = [[kept, lax.ppermute(sent, CORE, PAIR)] for kept, sent in zip(halves[:3], halves[3:6])]
    losses = halves[6] + streams[0][1][2048:]
    for stage in range(3):
        for turn in range(2):
            streams, losses = ring_round(streams, stage, turn, places, losses)
    grad_out = jnp.concatenate([part[:, :128] for (part,) in streams], axis=1)
    grad_in = jnp.concatenate([part[:, 128:] for (part,) in streams], axis=1)
    return new, grad_in, grad_out, losses[0, :BATCHES]


def on_device(state, target, land_mask, batch_map, diffusion, speed_x, speed_y, w_in, w_out):
    feats, rows_x, rows_y = state.shape
    field, x, strips = transported(state, diffusion, speed_x, speed_y)
    target, land_mask, batch_map, *_ = lax.optimization_barrier((target, land_mask, batch_map, *strips))
    local_cols = rows_x * rows_y
    total = local_cols * lax.axis_size(BX) * lax.axis_size(BY)
    new, grad_in, grad_out, batch_loss = network(
        x,
        field,
        target.reshape(feats, local_cols),
        land_mask,
        batch_map,
        w_in,
        w_out,
        total,
        ring_places(),
    )
    return (new.reshape(feats, rows_x, rows_y), grad_in, grad_out, batch_loss)


def solution(mesh):
    torus = Mesh(mesh.devices.reshape(2, 4, 4, 2, 2), BX + BY)
    return jax.shard_map(
        on_device,
        mesh=torus,
        in_specs=(P(None, BX, BY), P(None, BX, BY), P(BX, BY), P(BX, BY), P(), P(), P(), P(), P()),
        out_specs=(P(None, BX, BY), P(BX + BY, None), P(BX + BY, None), P()),
        check_vma=False,
    )
```
